32 devices in a mesh: groups: 2 (over y), tm: 4 (over z), head: 2 (over x), series: 2 (over core).
Axes of the slice: x: 2, y: 2, z: 4, core: 2. Of those that a mesh axis runs over, the one named last changes fastest.
Arguments:
- queries: bfloat16 [4, 4096, 1024], P(('groups', 'series'), 'tm', 'head'), parts along dimension 0, may hold values from -16 to 16
- key_vecs: bfloat16 [4, 4096, 1024], P(('groups', 'series'), 'tm', 'head'), parts along dimension 0, may hold values from -4 to 4
- value_vecs: bfloat16 [4, 4096, 1024], P(('groups', 'series'), 'tm', 'head'), parts along dimension 0, may hold values from -6 to 6
- out_grad: bfloat16 [4, 4096, 1024], P(('groups', 'series'), 'tm', 'head'), parts along dimension 0, may hold values from -6 to 6
- block_links: int32 [64, 4], P('tm'), may hold values from 0 to 63, as said below
- coarse_taps: float32 [2, 4, 4, 1024], P(None, None, None, 'head'), may hold values from 0.2 to 0.8
Outputs:
- attended: bfloat16 [4, 4096, 1024], P(('groups', 'series'), 'tm', 'head'), parts along dimension 0
- grad_query: bfloat16 [4, 4096, 1024], P(('groups', 'series'), 'tm', 'head'), parts along dimension 0
- grad_key: bfloat16 [4, 4096, 1024], P(('groups', 'series'), 'tm', 'head'), parts along dimension 0
- grad_value: bfloat16 [4, 4096, 1024], P(('groups', 'series'), 'tm', 'head'), parts along dimension 0
The draws below stay inside these ranges and needn't reach their ends.
There are 2 independent parts, one for each index of `groups`. The reference program is written for one: setup_inputs(seed, part) draws one part's arguments, and reference() takes and returns one part's arrays. A program takes and returns all parts, laid end to end along the dimension named above; an argument that names none is the same for every part. Nothing has to cross between parts.
Inputs may be any that keep to these rules, and one draw needn't show every extreme that they name: block_links[b, 0] lies in b - 2 .. b and block_links[b, 1] in b .. b + 2 (level-0 block ids); block_links[b, 2] is a level-1 block id within 2 of b // 4, block_links[b, 3] a level-2 block id within 2 of b // 16.
All inputs are finite; a program needn't handle non-finite values.
Results may differ from the reference program's by a relative error of at most 0.0095.
Values may be sent and summed in bfloat16 or wider, within the bound.
No kernel may reach another device: no remote copies, remote signals or barrier semaphores. Data moves between devices by JAX's collectives and lax.ppermute only.
A program may use at most 192 MiB of HBM per device.

```python
import math
import jax
import jax.numpy as jnp
from jax import lax

HEADS = 16
HEAD_DIM = 64
HF = 1024
BLOCK = 64
SERIES = 2
LEN = 4096
NB0 = 64


def draw_key_vecs(key, part):
    result = jnp.clip(jax.random.normal(jax.random.fold_in(key, 1), (SERIES, LEN, HF), jnp.float32), -4.0, 4.0)
    return result.astype(jnp.bfloat16)


def draw_queries(key, part):
    result = jnp.clip(jax.random.normal(jax.random.fold_in(key, 2), (SERIES, LEN, HF), jnp.float32), -4.0, 4.0)
    return result.astype(jnp.bfloat16)


def draw_block_links(key, part):
    block_index = jnp.arange(NB0, dtype=jnp.int32)
    step_left = jax.random.randint(jax.random.fold_in(key, 21), (NB0,), 1, 3, dtype=jnp.int32)
    step_right = jax.random.randint(jax.random.fold_in(key, 22), (NB0,), 1, 3, dtype=jnp.int32)
    left_link = jnp.maximum(block_index - step_left, 0)
    right_link = jnp.minimum(block_index + step_right, NB0 - 1)
    pick_one = jax.random.randint(jax.random.fold_in(key, 23), (NB0,), 0, 4, dtype=jnp.int32)
    shift_one = jnp.where(pick_one < 2, pick_one - 2, pick_one - 1)
    link_one = jnp.clip(block_index // 4 + shift_one, 0, NB0 // 4 - 1)
    pick_two = jax.random.randint(jax.random.fold_in(key, 24), (NB0,), 0, 4, dtype=jnp.int32)
    shift_two = jnp.where(pick_two < 2, pick_two - 2, pick_two - 1)
    link_two = jnp.clip(block_index // 16 + shift_two, 0, NB0 // 16 - 1)
    return jnp.stack([left_link, right_link, link_one, link_two], axis=1).astype(jnp.int32)


def level_of(key, shape, pieces, least, largest):
    loudness, own = 1.0, jax.random.fold_in(key, 6)
    for axis_at, parts in pieces:
        draws = jnp.exp(jax.random.uniform(jax.random.fold_in(own, axis_at), (parts,), jnp.float32, least / len(pieces), largest / len(pieces)))
        loudness = loudness * jnp.repeat(draws, shape[axis_at] // parts).reshape([-1 if axis == axis_at else 1 for axis in range(len(shape))])
    return loudness


def centred(key, shape, scale, limit, split=(), kind=jnp.bfloat16):
    values = jax.random.normal(key, shape, jnp.float32) * scale
    if len(split) > 0:
        values = level_of(key, shape, split, -0.22, 0.18) * values
    return jnp.clip(values, min=-limit, max=limit).astype(kind)


def setup_inputs(seed: int = 0, part: int = 0) -> dict:
    splits = jax.random.split(jax.random.key(seed), 7)
    own_keys = jax.random.split(jax.random.fold_in(splits[6], part), 7)
    queries = draw_queries(jax.random.fold_in(jax.random.fold_in(splits[6], part), 71), part)
    key_vecs = draw_key_vecs(jax.random.fold_in(jax.random.fold_in(splits[6], part), 71), part)
    value_vecs = centred(own_keys[2], (SERIES, LEN, HF), 1.0, 6.0, ((0, 2), (1, 4), (2, 2)))
    out_grad = centred(own_keys[3], (SERIES, LEN, HF), 1.0, 6.0, ((0, 2), (1, 4), (2, 2)))
    block_links = draw_block_links(jax.random.fold_in(splits[6], 71), part)
    coarse_taps = jnp.clip(0.2 + 0.6 * jax.random.uniform(splits[5], (2, 4, 4, HF), jnp.float32) ** level_of(splits[5], (2, 4, 4, HF), ((3, 2),), -0.2, 0.2), 0.2, 0.8)
    return dict(queries=queries, key_vecs=key_vecs, value_vecs=value_vecs, out_grad=out_grad, block_links=block_links, coarse_taps=coarse_taps)


def coarsen_step(fine_rows, tap_row):
    row_count = fine_rows.shape[0] // 4
    grouped = fine_rows.reshape(row_count, 4, fine_rows.shape[1]).astype(jnp.float32)
    return lax.optimization_barrier(jnp.sum(grouped * tap_row[None], axis=1)).astype(jnp.bfloat16)

def spread_back(coarse_grad, tap_row):
    row_count = coarse_grad.shape[0]
    return (coarse_grad[:, None, :] * tap_row[None]).reshape(row_count * 4, coarse_grad.shape[1])

def attend_block(q_block, keyvals, grad_block):
    score_scale = 1.0 / math.sqrt(HEAD_DIM)
    queries_h = q_block.reshape(-1, HEADS, HEAD_DIM).astype(jnp.float32)
    keys_h = keyvals[:, :HF].reshape(-1, HEADS, HEAD_DIM).astype(jnp.float32)
    values_h = keyvals[:, HF:].reshape(-1, HEADS, HEAD_DIM).astype(jnp.float32)
    grads_h = grad_block.reshape(-1, HEADS, HEAD_DIM).astype(jnp.float32)
    scores = jnp.einsum('qhd,khd->hqk', queries_h, keys_h) * score_scale
    row_max = lax.optimization_barrier(jnp.max(scores, axis=-1, keepdims=True))
    exponent = jnp.exp(scores - row_max)
    probs_f32 = exponent / lax.optimization_barrier(jnp.sum(exponent, axis=-1, keepdims=True))
    probs_b = lax.optimization_barrier(probs_f32.astype(jnp.bfloat16)).astype(jnp.float32)
    attended = jnp.einsum('hqk,khd->qhd', probs_b, values_h).reshape(-1, HF).astype(jnp.bfloat16)
    dprob = jnp.einsum('qhd,khd->hqk', grads_h, values_h)
    row_delta = lax.optimization_barrier(jnp.sum(probs_f32 * dprob, axis=-1, keepdims=True))
    dscore = lax.optimization_barrier((score_scale * probs_f32 * (dprob - row_delta)).astype(jnp.bfloat16)).astype(jnp.float32)
    grad_q = jnp.einsum('hqk,khd->qhd', dscore, keys_h).reshape(-1, HF).astype(jnp.bfloat16)
    grad_k = jnp.einsum('hqk,qhd->khd', dscore, queries_h).reshape(-1, HF)
    grad_v = jnp.einsum('hqk,qhd->khd', probs_b, grads_h).reshape(-1, HF)
    return (attended, grad_q, jnp.concatenate([grad_k, grad_v], axis=-1))

def one_series(queries, key_vecs, value_vecs, out_grad, block_links, tap_table):
    level_zero = jnp.concatenate([key_vecs, value_vecs], axis=-1)
    kv_width = level_zero.shape[1]
    levels_list = [level_zero]
    for section_idx in range(4):
        levels_list.append(coarsen_step(levels_list[-1], tap_table[section_idx]))
    blocks_zero = levels_list[0].reshape(-1, BLOCK, kv_width)
    blocks_one = levels_list[1].reshape(-1, BLOCK, kv_width)
    blocks_two = levels_list[2].reshape(-1, BLOCK, kv_width)
    upper_rows = jnp.concatenate([levels_list[3], levels_list[4]], axis=0)
    q_blocks = queries.reshape(-1, BLOCK, HF)
    g_blocks = out_grad.reshape(-1, BLOCK, HF)

    def block_step(totals, inputs):
        grad_zero, grad_one, grad_two, grad_up = totals
        q_block, g_block, link_row, block_index = inputs
        zero_ids = jnp.stack([block_index, link_row[0], link_row[1]])
        one_ids = jnp.stack([block_index // 4, link_row[2]])
        two_ids = jnp.stack([block_index // 16, link_row[3]])
        keyvals = jnp.concatenate([blocks_zero[zero_ids].reshape(-1, kv_width), blocks_one[one_ids].reshape(-1, kv_width), blocks_two[two_ids].reshape(-1, kv_width), upper_rows], axis=0)
        attended, grad_q, grad_kv = attend_block(q_block, keyvals, g_block)
        grad_zero = grad_zero.at[zero_ids].add(grad_kv[:3 * BLOCK].reshape(3, BLOCK, kv_width))
        grad_one = grad_one.at[one_ids].add(grad_kv[3 * BLOCK:5 * BLOCK].reshape(2, BLOCK, kv_width))
        grad_two = grad_two.at[two_ids].add(grad_kv[5 * BLOCK:7 * BLOCK].reshape(2, BLOCK, kv_width))
        grad_up = grad_up + grad_kv[7 * BLOCK:]
        return ((grad_zero, grad_one, grad_two, grad_up), (attended, grad_q))
    init_totals = (jnp.zeros(blocks_zero.shape, jnp.float32), jnp.zeros(blocks_one.shape, jnp.float32), jnp.zeros(blocks_two.shape, jnp.float32), jnp.zeros(upper_rows.shape, jnp.float32))
    block_ids = jnp.arange(NB0, dtype=jnp.int32)
    totals, outputs = lax.scan(block_step, init_totals, (q_blocks, g_blocks, block_links, block_ids))
    grad_zero, grad_one, grad_two, grad_up = totals
    three_rows = LEN // 64
    grad_three = grad_up[:three_rows]
    grad_four = grad_up[three_rows:]
    grad_three = grad_three + spread_back(grad_four, tap_table[3])
    grad_two = grad_two.reshape(-1, kv_width) + spread_back(grad_three, tap_table[2])
    grad_one = grad_one.reshape(-1, kv_width) + spread_back(grad_two, tap_table[1])
    grad_zero = grad_zero.reshape(-1, kv_width) + spread_back(grad_one, tap_table[0])
    attended = outputs[0].reshape(LEN, HF)
    grad_query = outputs[1].reshape(LEN, HF)
    return (attended, grad_query, grad_zero[:, :HF].astype(jnp.bfloat16), grad_zero[:, HF:].astype(jnp.bfloat16))

def reference(queries, key_vecs, value_vecs, out_grad, block_links, coarse_taps):
    tap_table = jnp.concatenate([coarse_taps[0], coarse_taps[1]], axis=-1)

    def per_series(operands):
        return one_series(operands[0], operands[1], operands[2], operands[3], block_links, tap_table)
    attended, grad_query, grad_key, grad_value = lax.map(per_series, (queries, key_vecs, value_vecs, out_grad))
    return (attended, grad_query, grad_key, grad_value)
```

```python
import jax
import jax.numpy as jnp
from jax import lax
from jax.experimental import pallas as pl
from jax.experimental.pallas import tpu as pltpu
from jax.sharding import PartitionSpec as P

HEAD_DIM = 64
BLOCK = 64
RIM = 2 * BLOCK
NEAR = 7 * BLOCK
VMEM_LIMIT = 56 * 1024 * 1024
F32 = jnp.float32
BF16 = jnp.bfloat16


def dot(a, b, ca, cb):
    return lax.dot_general(a, b, (((ca,), (cb,)), ((), ())), preferred_element_type=F32)


LANES = 128


def widen(scratch, value, at=0):
    for c in range(value.shape[1] // LANES):
        scratch[c, pl.ds(at, value.shape[0]), :] = value[:, c * LANES : (c + 1) * LANES].astype(F32)


def coarse_rows(scratch, count, taps_ref, which, depth):
    parts = []
    for c in range(scratch.shape[0]):
        lanes = slice(c * LANES, (c + 1) * LANES)
        total = None
        for t in range(4):
            part = scratch[c, pl.ds(t, count, stride=4), :] * taps_ref[which, depth, t : t + 1, lanes]
            total = part if total is None else total + part
        parts.append(total)
    return jnp.concatenate(parts, axis=1)


def spread_rows(scratch, coarse, taps_ref, which, depth):
    count = coarse.shape[0]
    parts = []
    for c in range(scratch.shape[0]):
        lanes = slice(c * LANES, (c + 1) * LANES)
        for t in range(4):
            scratch[c, pl.ds(t, count, stride=4), :] = (
                coarse[:, lanes] * taps_ref[which, depth, t : t + 1, lanes]
            )
        parts.append(scratch[c, : 4 * count, :])
    return jnp.concatenate(parts, axis=1)


def coarsen_kernel(k_ref, v_ref, taps_ref, left_ref, right_ref, two_ref, far_ref, wide, mid, low):
    rows = k_ref.shape[0]
    one, two, three = rows // 4, rows // 16, rows // 64
    for which, own in ((0, k_ref), (1, v_ref)):
        left_ref[which, :RIM] = own[:RIM]
        right_ref[which, :RIM] = own[rows - RIM :]
        widen(wide, own[...])
        level_one = coarse_rows(wide, one, taps_ref, which, 0).astype(BF16)
        left_ref[which, RIM : 2 * RIM] = level_one[:RIM]
        right_ref[which, RIM : 2 * RIM] = level_one[one - RIM :]
        widen(mid, level_one)
        level_two = coarse_rows(mid, two, taps_ref, which, 1).astype(BF16)
        widen(low, level_two)
        level_three = coarse_rows(low, three, taps_ref, which, 2).astype(BF16)
        for target, at in ((left_ref, 2 * RIM), (right_ref, 2 * RIM), (two_ref, 0)):
            target[which, at : at + two] = level_two
            target[which, at + two : at + two + three] = level_three
        far_ref[which] = level_three


def attend_kernel(
    tm_count,
    near_two,
    pos_ref,
    links_ref,
    q_ref,
    g_ref,
    k_ref,
    v_ref,
    taps_ref,
    left_ref,
    right_ref,
    below_ref,
    above_ref,
    *rest,
):
    twos = rest[: len(near_two)]
    far_ref = rest[len(near_two)]
    (att_ref, gq_ref, g_zero, g_one, g_two, to_below, to_above) = rest[len(near_two) + 1 :][:7]
    to_twos = rest[len(near_two) + 8 :][: len(near_two)]
    to_far, k_pool, v_pool, k_acc, v_acc, three_f32, fold = rest[2 * len(near_two) + 8 :]
    step = pl.program_id(1)
    last = pl.num_programs(1) - 1
    position = pos_ref[0]
    rows = k_ref.shape[0]
    width = k_ref.shape[1]
    heads = width // HEAD_DIM
    blocks = rows // BLOCK
    one_rows = rows // 4
    base_one = rows + 2 * RIM
    base_two = base_one + one_rows + 2 * RIM
    base_three = base_two + tm_count * BLOCK
    three = rows // 64
    base_four = base_three + tm_count * three
    four_rows = tm_count * three // 4
    upper = tm_count * three + four_rows

    @pl.when(step == 0)
    def _():
        for which, pool, own in ((0, k_pool, k_ref), (1, v_pool, v_ref)):
            pool[:RIM] = below_ref[which, :RIM]
            pool[RIM : RIM + rows] = own[...]
            pool[RIM + rows : base_one] = above_ref[which, :RIM]
            pool[base_one : base_one + RIM] = below_ref[which, RIM : 2 * RIM]
            pool[base_one + RIM : base_one + 2 * RIM] = left_ref[which, RIM : 2 * RIM]
            pool[base_two - 2 * RIM : base_two - RIM] = right_ref[which, RIM : 2 * RIM]
            pool[base_two - RIM : base_two] = above_ref[which, RIM : 2 * RIM]

            def place(source, at, owner):
                spot = pl.multiple_of(base_two + owner * BLOCK, BLOCK)
                pool[pl.ds(spot, BLOCK), :] = source[which, at : at + BLOCK]
                spot_three = pl.multiple_of(owner * three, three)
                widen(three_f32, source[which, at + BLOCK : at + BLOCK + three], spot_three)

            if tm_count == 4:

                @pl.when((position == 0) | (position == 3))
                def _():
                    spot = pl.multiple_of((3 - position) * three, three)
                    widen(three_f32, far_ref[which], spot)

            else:
                for owner in range(tm_count):
                    widen(three_f32, far_ref[owner, which], owner * three)
            place(left_ref, 2 * RIM, position)

            @pl.when(position > 0)
            def _():
                place(below_ref, 2 * RIM, position - 1)

            @pl.when(position < tm_count - 1)
            def _():
                place(above_ref, 2 * RIM, position + 1)

            for source, shift in zip(twos, near_two):
                if shift is None:
                    place(source, 0, lax.rem(position + 2, 4))
                else:

                    @pl.when((position + shift >= 0) & (position + shift < tm_count))
                    def _():
                        place(source, 0, position + shift)

            for c in range(width // LANES):
                pool[base_three:base_four, c * LANES : (c + 1) * LANES] = three_f32[c].astype(BF16)
            pool[base_four : base_four + four_rows] = coarse_rows(
                three_f32, four_rows, taps_ref, which, 3
            ).astype(BF16)
        k_acc[...] = jnp.zeros_like(k_acc)
        v_acc[...] = jnp.zeros_like(v_acc)

    own = position * blocks + step
    first_zero = position * blocks - 2
    first_one = position * (blocks // 4) - 2
    spots = [
        (step + 2) * BLOCK,
        (links_ref[step, 0] - first_zero) * BLOCK,
        (links_ref[step, 1] - first_zero) * BLOCK,
        base_one + (own // 4 - first_one) * BLOCK,
        base_one + (links_ref[step, 2] - first_one) * BLOCK,
        base_two + (own // 16) * BLOCK,
        base_two + links_ref[step, 3] * BLOCK,
    ]
    spots = [pl.multiple_of(spot, BLOCK) for spot in spots]

    def gathered(pool):
        parts = [pool[pl.ds(spot, BLOCK), :] for spot in spots]
        return jnp.concatenate(parts + [pool[base_three : base_three + upper]], axis=0)

    stacked = heads * BLOCK
    row_head = lax.broadcasted_iota(jnp.int32, (stacked, width), 0) // BLOCK
    lane_head = lax.broadcasted_iota(jnp.int32, (stacked, width), 1) // HEAD_DIM
    same = row_head == lane_head

    def diagonal(block):
        wide = jnp.concatenate([block] * heads, axis=0)
        return jnp.where(same, wide, 0.0).astype(BF16)

    q_diag = diagonal(q_ref[...].astype(F32) * 0.125)
    g_diag = diagonal(g_ref[...].astype(F32))
    keys = gathered(k_pool)
    values = gathered(v_pool)
    scores = dot(keys, q_diag, 1, 1)
    row_max = jnp.max(scores, axis=0, keepdims=True)
    exponent = jnp.exp(scores - row_max)
    probs = exponent * (1.0 / jnp.sum(exponent, axis=0, keepdims=True))
    probs_b = probs.astype(BF16)
    dprob = dot(values, g_diag, 1, 1)
    row_delta = jnp.sum(probs * dprob, axis=0, keepdims=True)
    dscore = (probs * (dprob - row_delta)).astype(BF16)
    pick = (
        lax.broadcasted_iota(jnp.int32, (BLOCK, stacked), 1) % BLOCK
        == lax.broadcasted_iota(jnp.int32, (BLOCK, stacked), 0)
    )
    pick = jnp.where(pick, 1.0, 0.0).astype(BF16)
    same_t = (
        lax.broadcasted_iota(jnp.int32, (width, stacked), 0) // HEAD_DIM
        == lax.broadcasted_iota(jnp.int32, (width, stacked), 1) // BLOCK
    )

    def folded(product):
        kept = jnp.where(same_t, product, 0.0).astype(BF16)
        return dot(pick, kept, 1, 1).astype(BF16)

    att_ref[...] = folded(dot(values, probs_b, 0, 0))
    gq_ref[...] = folded(dot(keys, dscore, 0, 0) * 0.125)
    grad_k = dot(dscore, q_diag, 1, 0)
    grad_v = dot(probs_b, g_diag, 1, 0)
    for acc, grad in ((k_acc, grad_k), (v_acc, grad_v)):
        for n, spot in enumerate(spots):
            acc[pl.ds(spot, BLOCK), :] += grad[n * BLOCK : (n + 1) * BLOCK]
        acc[base_three : base_three + upper] += grad[NEAR:]

    @pl.when(step == last)
    def _():
        for which, acc in ((0, k_acc), (1, v_acc)):
            four = acc[base_four : base_four + four_rows]
            acc[base_three:base_four] += spread_rows(fold, four, taps_ref, which, 3)
            acc[base_two:base_three] += spread_rows(fold, acc[base_three:base_four], taps_ref, which, 2)
            g_zero[which] = acc[RIM : RIM + rows]
            g_one[which] = acc[base_one + RIM : base_two - RIM]

            def slot(owner):
                return acc[pl.ds(pl.multiple_of(base_two + owner * BLOCK, BLOCK), BLOCK), :]

            g_two[which] = slot(position)
            to_below[which, :RIM] = acc[:RIM].astype(BF16)
            to_below[which, RIM : 2 * RIM] = acc[base_one : base_one + RIM].astype(BF16)
            to_below[which, 2 * RIM :] = slot(jnp.maximum(position - 1, 0)).astype(BF16)
            to_above[which, :RIM] = acc[RIM + rows : base_one].astype(BF16)
            to_above[which, RIM : 2 * RIM] = acc[base_two - RIM : base_two].astype(BF16)
            to_above[which, 2 * RIM :] = slot(jnp.minimum(position + 1, tm_count - 1)).astype(BF16)
            for target, shift in zip(to_twos, near_two):
                if shift is None:
                    target[which] = slot(lax.rem(position + 2, 4)).astype(BF16)
                else:
                    target[which] = slot(jnp.clip(position + shift, 0, tm_count - 1)).astype(BF16)
            if tm_count == 4:
                spot = pl.multiple_of(base_three + (3 - position) * three, three)
                to_far[which] = acc[pl.ds(spot, three), :].astype(BF16)
            else:
                for owner in range(tm_count):
                    part = acc[base_three + owner * three : base_three + (owner + 1) * three]
                    is_far = (position - owner > 2) | (owner - position > 2)
                    to_far[owner, which] = jnp.where(is_far, part, 0.0).astype(BF16)


def finish_kernel(two_count, g_zero, g_one, g_two, taps_ref, below_ref, above_ref, *rest):
    twos = rest[:two_count]
    far_ref, gk_ref, gv_ref, zero, one, two = rest[two_count:]
    rows = g_zero.shape[1]
    for which, out in ((0, gk_ref), (1, gv_ref)):
        total = g_two[which] + below_ref[which, 2 * RIM :].astype(F32) + above_ref[which, 2 * RIM :].astype(F32)
        for extra in twos:
            total += extra[which].astype(F32)
        total += spread_rows(two, far_ref[which].astype(F32), taps_ref, which, 2)
        ones = spread_rows(one, total, taps_ref, which, 1) + g_one[which]
        ones = jnp.concatenate(
            [
                ones[:RIM] + below_ref[which, RIM : 2 * RIM].astype(F32),
                ones[RIM : ones.shape[0] - RIM],
                ones[ones.shape[0] - RIM :] + above_ref[which, RIM : 2 * RIM].astype(F32),
            ][:: 1 if ones.shape[0] > 2 * RIM else 2],
            axis=0,
        )
        zeros = spread_rows(zero, ones, taps_ref, which, 0) + g_zero[which]
        out[:RIM] = (zeros[:RIM] + below_ref[which, :RIM].astype(F32)).astype(BF16)
        out[RIM : rows - RIM] = zeros[RIM : rows - RIM].astype(BF16)
        out[rows - RIM :] = (zeros[rows - RIM :] + above_ref[which, :RIM].astype(F32)).astype(BF16)


def shifted(x, shift):
    count = lax.axis_size("tm")
    pairs = [(i, i + shift) for i in range(count) if 0 <= i + shift < count]
    return lax.ppermute(x, "tm", pairs)


def shards(queries, key_vecs, value_vecs, out_grad, block_links, coarse_taps):
    queries, key_vecs, value_vecs, out_grad = (x[0] for x in (queries, key_vecs, value_vecs, out_grad))
    rows, features = queries.shape
    tm_count = lax.axis_size("tm")
    position = lax.axis_index("tm").astype(jnp.int32).reshape(1)
    width = min(features, 256)
    parts = features // width
    blocks = rows // BLOCK
    two, three = rows // 16, rows // 64
    pack = 2 * RIM + two + three
    params = pltpu.CompilerParams(vmem_limit_bytes=VMEM_LIMIT)

    def plain(*shape):
        lead = len(shape) - 1
        return pl.BlockSpec(shape[:-1] + (width,), lambda g: (0,) * lead + (g,))

    def shape_of(*shape, dtype=BF16):
        return jax.ShapeDtypeStruct(shape, dtype)

    taps_spec = plain(2, 4, 4, features)
    left, right, near, far = pl.pallas_call(
        coarsen_kernel,
        grid=(parts,),
        in_specs=[plain(rows, features), plain(rows, features), taps_spec],
        out_specs=[
            plain(2, pack, features),
            plain(2, pack, features),
            plain(2, two + three, features),
            plain(2, three, features),
        ],
        out_shape=[
            shape_of(2, pack, features),
            shape_of(2, pack, features),
            shape_of(2, two + three, features),
            shape_of(2, three, features),
        ],
        scratch_shapes=[
            pltpu.VMEM((width // LANES, rows, LANES), F32),
            pltpu.VMEM((width // LANES, rows // 4, LANES), F32),
            pltpu.VMEM((width // LANES, two, LANES), F32),
        ],
        compiler_params=params,
        name="coarsen",
    )(key_vecs, value_vecs, coarse_taps)

    below = shifted(right, 1)
    above = shifted(left, -1)
    if tm_count == 4:
        near_two = (None,)
        twos = [lax.ppermute(near, "tm", [(i, (i + 2) % 4) for i in range(4)])]
        far_in = lax.ppermute(far, "tm", [(0, 3), (3, 0)])
        far_shape = (2, three, features)
    else:
        near_two = (-2, 2)
        twos = [shifted(near, 2), shifted(near, -2)]
        far_in = lax.all_gather(far, "tm")
        far_shape = (tm_count, 2, three, features)

    def held(*shape):
        lead = len(shape) - 1
        return pl.BlockSpec(shape[:-1] + (width,), lambda g, i, *_: (0,) * lead + (g,))

    row_spec = pl.BlockSpec((BLOCK, width), lambda g, i, *_: (i, g))
    pool_rows = rows + 2 * RIM + rows // 4 + 2 * RIM + tm_count * (BLOCK + three) + tm_count * three // 4
    back = 2 * RIM + two
    grads = pl.pallas_call(
        lambda *refs: attend_kernel(tm_count, near_two, *refs),
        grid_spec=pltpu.PrefetchScalarGridSpec(
            num_scalar_prefetch=2,
            grid=(parts, blocks),
            in_specs=[
                row_spec,
                row_spec,
                held(rows, features),
                held(rows, features),
                held(2, 4, 4, features),
            ]
            + [held(2, pack, features)] * 4
            + [held(2, two + three, features)] * len(twos)
            + [held(*far_shape)],
            out_specs=[
                row_spec,
                row_spec,
                held(2, rows, features),
                held(2, rows // 4, features),
                held(2, two, features),
                held(2, back, features),
                held(2, back, features),
            ]
            + [held(2, two, features)] * len(twos)
            + [held(*far_shape)],
            scratch_shapes=[
                pltpu.VMEM((pool_rows, width), BF16),
                pltpu.VMEM((pool_rows, width), BF16),
                pltpu.VMEM((pool_rows, width), F32),
                pltpu.VMEM((pool_rows, width), F32),
                pltpu.VMEM((width // LANES, tm_count * three, LANES), F32),
                pltpu.VMEM((width // LANES, tm_count * BLOCK, LANES), F32),
            ],
        ),
        out_shape=[
            shape_of(rows, features),
            shape_of(rows, features),
            shape_of(2, rows, features, dtype=F32),
            shape_of(2, rows // 4, features, dtype=F32),
            shape_of(2, two, features, dtype=F32),
            shape_of(2, back, features),
            shape_of(2, back, features),
        ]
        + [shape_of(2, two, features)] * len(twos)
        + [shape_of(*far_shape)],
        compiler_params=params,
        name="attend",
    )(
        position,
        block_links,
        queries,
        out_grad,
        key_vecs,
        value_vecs,
        coarse_taps,
        left,
        right,
        below,
        above,
        *twos,
        far_in,
    )
    attended, grad_query, g_zero, g_one, g_two, to_below, to_above = grads[:7]
    to_twos = grads[7 : 7 + len(twos)]
    to_far = grads[-1]
    from_below = shifted(to_above, 1)
    from_above = shifted(to_below, -1)
    if tm_count == 4:
        from_twos = [lax.ppermute(to_twos[0], "tm", [(i, (i + 2) % 4) for i in range(4)])]
        from_far = lax.ppermute(to_far, "tm", [(0, 3), (3, 0)])
    else:
        from_twos = [shifted(grad, shift) for grad, shift in zip(to_twos, near_two)]
        from_far = lax.psum_scatter(to_far, "tm", scatter_dimension=0)
    grad_key, grad_value = pl.pallas_call(
        lambda *refs: finish_kernel(len(twos), *refs),
        grid=(parts,),
        in_specs=[
            plain(2, rows, features),
            plain(2, rows // 4, features),
            plain(2, two, features),
            taps_spec,
            plain(2, back, features),
            plain(2, back, features),
        ]
        + [plain(2, two, features)] * len(twos)
        + [plain(2, three, features)],
        out_specs=[plain(rows, features), plain(rows, features)],
        out_shape=[shape_of(rows, features), shape_of(rows, features)],
        scratch_shapes=[
            pltpu.VMEM((width // LANES, rows, LANES), F32),
            pltpu.VMEM((width // LANES, rows // 4, LANES), F32),
            pltpu.VMEM((width // LANES, two, LANES), F32),
        ],
        compiler_params=params,
        name="finish",
    )(g_zero, g_one, g_two, coarse_taps, from_below, from_above, *from_twos, from_far)
    return tuple(x[None] for x in (attended, grad_query, grad_key, grad_value))


def solution(mesh):
    spec = P(("groups", "series"), "tm", "head")
    in_specs = (spec, spec, spec, spec, P("tm", None), P(None, None, None, "head"))
    return jax.shard_map(shards, mesh=mesh, in_specs=in_specs, out_specs=(spec,) * 4, check_vma=False)
```

```python
import jax
import jax.numpy as jnp
from jax import lax
from jax.experimental import pallas as pl
from jax.experimental.pallas import tpu as pltpu
from jax.sharding import PartitionSpec as P

HEAD_DIM = 64
BLOCK = 64
RIM = 2 * BLOCK
NEAR = 7 * BLOCK
PER_STEP = 8
VMEM_LIMIT = 56 * 1024 * 1024
F32 = jnp.float32
BF16 = jnp.bfloat16


def dot(a, b, ca, cb):
    return lax.dot_general(a, b, (((ca,), (cb,)), ((), ())), preferred_element_type=F32)


LANES = 128


def widen(scratch, value, at=0):
    for c in range(value.shape[1] // LANES):
        scratch[c, pl.ds(at, value.shape[0]), :] = value[:, c * LANES : (c + 1) * LANES].astype(F32)


def coarse_rows(scratch, count, taps_ref, which, depth):
    parts = []
    for c in range(scratch.shape[0]):
        lanes = slice(c * LANES, (c + 1) * LANES)
        total = None
        for t in range(4):
            part = scratch[c, pl.ds(t, count, stride=4), :] * taps_ref[which, depth, t : t + 1, lanes]
            total = part if total is None else total + part
        parts.append(total)
    return jnp.concatenate(parts, axis=1)


def spread_rows(scratch, coarse, taps_ref, which, depth):
    count = coarse.shape[0]
    parts = []
    for c in range(scratch.shape[0]):
        lanes = slice(c * LANES, (c + 1) * LANES)
        for t in range(4):
            scratch[c, pl.ds(t, count, stride=4), :] = (
                coarse[:, lanes] * taps_ref[which, depth, t : t + 1, lanes]
            )
        parts.append(scratch[c, : 4 * count, :])
    return jnp.concatenate(parts, axis=1)


def coarsen_kernel(k_ref, v_ref, taps_ref, left_ref, right_ref, two_ref, far_ref, wide, mid, low):
    rows = k_ref.shape[0]
    one, two, three = rows // 4, rows // 16, rows // 64
    for which, own in ((0, k_ref), (1, v_ref)):
        left_ref[which, :RIM] = own[:RIM]
        right_ref[which, :RIM] = own[rows - RIM :]
        widen(wide, own[...])
        level_one = coarse_rows(wide, one, taps_ref, which, 0).astype(BF16)
        left_ref[which, RIM : 2 * RIM] = level_one[:RIM]
        right_ref[which, RIM : 2 * RIM] = level_one[one - RIM :]
        widen(mid, level_one)
        level_two = coarse_rows(mid, two, taps_ref, which, 1).astype(BF16)
        widen(low, level_two)
        level_three = coarse_rows(low, three, taps_ref, which, 2).astype(BF16)
        for target, at in ((left_ref, 2 * RIM), (right_ref, 2 * RIM), (two_ref, 0)):
            target[which, at : at + two] = level_two
            target[which, at + two : at + two + three] = level_three
        far_ref[which] = level_three


def attend_kernel(
    tm_count,
    near_two,
    pos_ref,
    links_ref,
    q_ref,
    g_ref,
    k_ref,
    v_ref,
    taps_ref,
    left_ref,
    right_ref,
    below_ref,
    above_ref,
    *rest,
):
    twos = rest[: len(near_two)]
    far_ref = rest[len(near_two)]
    (att_ref, gq_ref, g_zero, g_one, g_two, to_below, to_above) = rest[len(near_two) + 1 :][:7]
    to_twos = rest[len(near_two) + 8 :][: len(near_two)]
    to_far, k_pool, v_pool, k_acc, v_acc, three_f32, fold = rest[2 * len(near_two) + 8 :]
    step = pl.program_id(1)
    last = pl.num_programs(1) - 1
    position = pos_ref[0]
    rows = k_ref.shape[0]
    width = k_ref.shape[1]
    heads = width // HEAD_DIM
    blocks = rows // BLOCK
    one_rows = rows // 4
    base_one = rows + 2 * RIM
    base_two = base_one + one_rows + 2 * RIM
    base_three = base_two + tm_count * BLOCK
    three = rows // 64
    base_four = base_three + tm_count * three
    four_rows = tm_count * three // 4
    upper = tm_count * three + four_rows

    @pl.when(step == 0)
    def _():
        for which, pool, own in ((0, k_pool, k_ref), (1, v_pool, v_ref)):
            pool[:RIM] = below_ref[which, :RIM]
            pool[RIM : RIM + rows] = own[...]
            pool[RIM + rows : base_one] = above_ref[which, :RIM]
            pool[base_one : base_one + RIM] = below_ref[which, RIM : 2 * RIM]
            pool[base_one + RIM : base_one + 2 * RIM] = left_ref[which, RIM : 2 * RIM]
            pool[base_two - 2 * RIM : base_two - RIM] = right_ref[which, RIM : 2 * RIM]
            pool[base_two - RIM : base_two] = above_ref[which, RIM : 2 * RIM]

            def place(source, at, owner):
                spot = pl.multiple_of(base_two + owner * BLOCK, BLOCK)
                pool[pl.ds(spot, BLOCK), :] = source[which, at : at + BLOCK]
                spot_three = pl.multiple_of(owner * three, three)
                widen(three_f32, source[which, at + BLOCK : at + BLOCK + three], spot_three)

            if tm_count == 4:

                @pl.when((position == 0) | (position == 3))
                def _():
                    spot = pl.multiple_of((3 - position) * three, three)
                    widen(three_f32, far_ref[which], spot)

            else:
                for owner in range(tm_count):
                    widen(three_f32, far_ref[owner, which], owner * three)
            place(left_ref, 2 * RIM, position)

            @pl.when(position > 0)
            def _():
                place(below_ref, 2 * RIM, position - 1)

            @pl.when(position < tm_count - 1)
            def _():
                place(above_ref, 2 * RIM, position + 1)

            for source, shift in zip(twos, near_two):
                if shift is None:
                    place(source, 0, lax.rem(position + 2, 4))
                else:

                    @pl.when((position + shift >= 0) & (position + shift < tm_count))
                    def _():
                        place(source, 0, position + shift)

            for c in range(width // LANES):
                pool[base_three:base_four, c * LANES : (c + 1) * LANES] = three_f32[c].astype(BF16)
            pool[base_four : base_four + four_rows] = coarse_rows(
                three_f32, four_rows, taps_ref, which, 3
            ).astype(BF16)
        k_acc[...] = jnp.zeros_like(k_acc)
        v_acc[...] = jnp.zeros_like(v_acc)

    first_zero = position * blocks - 2
    first_one = position * (blocks // 4) - 2
    stacked = heads * BLOCK
    row_head = lax.broadcasted_iota(jnp.int32, (stacked, width), 0) // BLOCK
    lane_head = lax.broadcasted_iota(jnp.int32, (stacked, width), 1) // HEAD_DIM
    same = row_head == lane_head

    def diagonal(block):
        wide = jnp.concatenate([block] * heads, axis=0)
        return jnp.where(same, wide, 0.0).astype(BF16)

    low_lanes = lax.broadcasted_iota(jnp.int32, (BLOCK, LANES), 1) < HEAD_DIM

    def folded(product):
        parts = []
        for pair in range(width // LANES):
            span = slice(pair * LANES, (pair + 1) * LANES)
            turned = product[span, span].T
            parts.append(jnp.where(low_lanes, turned[:BLOCK], turned[BLOCK:]))
        return jnp.concatenate(parts, axis=1).astype(BF16)

    def products(unit):
        at = unit * BLOCK
        block = step * PER_STEP + unit
        own = position * blocks + block
        spots = [
            (block + 2) * BLOCK,
            (links_ref[block, 0] - first_zero) * BLOCK,
            (links_ref[block, 1] - first_zero) * BLOCK,
            base_one + (own // 4 - first_one) * BLOCK,
            base_one + (links_ref[block, 2] - first_one) * BLOCK,
            base_two + (own // 16) * BLOCK,
            base_two + links_ref[block, 3] * BLOCK,
        ]
        spots = [pl.multiple_of(spot, BLOCK) for spot in spots]

        def gathered(pool):
            parts = [pool[pl.ds(spot, BLOCK), :] for spot in spots]
            return jnp.concatenate(parts + [pool[base_three : base_three + upper]], axis=0)

        q_diag = diagonal(q_ref[at : at + BLOCK].astype(F32) * 0.125)
        g_diag = diagonal(g_ref[at : at + BLOCK].astype(F32))
        keys = gathered(k_pool)
        values = gathered(v_pool)
        scores = dot(keys, q_diag, 1, 1)
        dprob = dot(values, g_diag, 1, 1)
        return at, spots, q_diag, g_diag, keys, values, scores, dprob

    def softmax(state):
        at, spots, q_diag, g_diag, keys, values, scores, dprob = state
        row_max = jnp.max(scores, axis=0, keepdims=True)
        exponent = jnp.exp(scores - row_max)
        probs = exponent * (1.0 / jnp.sum(exponent, axis=0, keepdims=True))
        probs_b = probs.astype(BF16)
        row_delta = jnp.sum(probs * dprob, axis=0, keepdims=True)
        dscore = (probs * (dprob - row_delta)).astype(BF16)
        return at, spots, q_diag, g_diag, keys, values, probs_b, dscore

    def gradients(state):
        at, spots, q_diag, g_diag, keys, values, probs_b, dscore = state
        att_ref[at : at + BLOCK] = folded(dot(values, probs_b, 0, 0))
        gq_ref[at : at + BLOCK] = folded(dot(keys, dscore, 0, 0) * 0.125)
        grad_k = dot(dscore, q_diag, 1, 0)
        grad_v = dot(probs_b, g_diag, 1, 0)
        for acc, grad in ((k_acc, grad_k), (v_acc, grad_v)):
            for n, spot in enumerate(spots):
                acc[pl.ds(spot, BLOCK), :] += grad[n * BLOCK : (n + 1) * BLOCK]
            acc[base_three : base_three + upper] += grad[NEAR:]

    ahead = products(0)
    behind = None
    for unit in range(PER_STEP):
        now = ahead
        if unit + 1 < PER_STEP:
            ahead = products(unit + 1)
        if behind is not None:
            gradients(behind)
        behind = softmax(now)
    gradients(behind)

    @pl.when(step == last)
    def _():
        for which, acc in ((0, k_acc), (1, v_acc)):
            four = acc[base_four : base_four + four_rows]
            acc[base_three:base_four] += spread_rows(fold, four, taps_ref, which, 3)
            acc[base_two:base_three] += spread_rows(fold, acc[base_three:base_four], taps_ref, which, 2)
            g_zero[which] = acc[RIM : RIM + rows]
            g_one[which] = acc[base_one + RIM : base_two - RIM]

            def slot(owner):
                return acc[pl.ds(pl.multiple_of(base_two + owner * BLOCK, BLOCK), BLOCK), :]

            g_two[which] = slot(position)
            to_below[which, :RIM] = acc[:RIM].astype(BF16)
            to_below[which, RIM : 2 * RIM] = acc[base_one : base_one + RIM].astype(BF16)
            to_below[which, 2 * RIM :] = slot(jnp.maximum(position - 1, 0)).astype(BF16)
            to_above[which, :RIM] = acc[RIM + rows : base_one].astype(BF16)
            to_above[which, RIM : 2 * RIM] = acc[base_two - RIM : base_two].astype(BF16)
            to_above[which, 2 * RIM :] = slot(jnp.minimum(position + 1, tm_count - 1)).astype(BF16)
            for target, shift in zip(to_twos, near_two):
                if shift is None:
                    target[which] = slot(lax.rem(position + 2, 4)).astype(BF16)
                else:
                    target[which] = slot(jnp.clip(position + shift, 0, tm_count - 1)).astype(BF16)
            if tm_count == 4:
                spot = pl.multiple_of(base_three + (3 - position) * three, three)
                to_far[which] = acc[pl.ds(spot, three), :].astype(BF16)
            else:
                for owner in range(tm_count):
                    part = acc[base_three + owner * three : base_three + (owner + 1) * three]
                    is_far = (position - owner > 2) | (owner - position > 2)
                    to_far[owner, which] = jnp.where(is_far, part, 0.0).astype(BF16)


def finish_kernel(two_count, g_zero, g_one, g_two, taps_ref, below_ref, above_ref, *rest):
    twos = rest[:two_count]
    far_ref, gk_ref, gv_ref, zero, one, two = rest[two_count:]
    rows = g_zero.shape[1]
    for which, out in ((0, gk_ref), (1, gv_ref)):
        total = g_two[which] + below_ref[which, 2 * RIM :].astype(F32) + above_ref[which, 2 * RIM :].astype(F32)
        for extra in twos:
            total += extra[which].astype(F32)
        total += spread_rows(two, far_ref[which].astype(F32), taps_ref, which, 2)
        ones = spread_rows(one, total, taps_ref, which, 1) + g_one[which]
        ones = jnp.concatenate(
            [
                ones[:RIM] + below_ref[which, RIM : 2 * RIM].astype(F32),
                ones[RIM : ones.shape[0] - RIM],
                ones[ones.shape[0] - RIM :] + above_ref[which, RIM : 2 * RIM].astype(F32),
            ][:: 1 if ones.shape[0] > 2 * RIM else 2],
            axis=0,
        )
        zeros = spread_rows(zero, ones, taps_ref, which, 0) + g_zero[which]
        out[:RIM] = (zeros[:RIM] + below_ref[which, :RIM].astype(F32)).astype(BF16)
        out[RIM : rows - RIM] = zeros[RIM : rows - RIM].astype(BF16)
        out[rows - RIM :] = (zeros[rows - RIM :] + above_ref[which, :RIM].astype(F32)).astype(BF16)


def shifted(x, shift):
    count = lax.axis_size("tm")
    pairs = [(i, i + shift) for i in range(count) if 0 <= i + shift < count]
    return lax.ppermute(x, "tm", pairs)


def shards(queries, key_vecs, value_vecs, out_grad, block_links, coarse_taps):
    queries, key_vecs, value_vecs, out_grad = (x[0] for x in (queries, key_vecs, value_vecs, out_grad))
    rows, features = queries.shape
    tm_count = lax.axis_size("tm")
    position = lax.axis_index("tm").astype(jnp.int32).reshape(1)
    width = min(features, 256)
    parts = features // width
    blocks = rows // BLOCK
    two, three = rows // 16, rows // 64
    pack = 2 * RIM + two + three
    params = pltpu.CompilerParams(vmem_limit_bytes=VMEM_LIMIT)

    def plain(*shape):
        lead = len(shape) - 1
        return pl.BlockSpec(shape[:-1] + (width,), lambda g: (0,) * lead + (g,))

    def shape_of(*shape, dtype=BF16):
        return jax.ShapeDtypeStruct(shape, dtype)

    taps_spec = plain(2, 4, 4, features)
    left, right, near, far = pl.pallas_call(
        coarsen_kernel,
        grid=(parts,),
        in_specs=[plain(rows, features), plain(rows, features), taps_spec],
        out_specs=[
            plain(2, pack, features),
            plain(2, pack, features),
            plain(2, two + three, features),
            plain(2, three, features),
        ],
        out_shape=[
            shape_of(2, pack, features),
            shape_of(2, pack, features),
            shape_of(2, two + three, features),
            shape_of(2, three, features),
        ],
        scratch_shapes=[
            pltpu.VMEM((width // LANES, rows, LANES), F32),
            pltpu.VMEM((width // LANES, rows // 4, LANES), F32),
            pltpu.VMEM((width // LANES, two, LANES), F32),
        ],
        compiler_params=params,
        name="coarsen",
    )(key_vecs, value_vecs, coarse_taps)

    below = shifted(right, 1)
    above = shifted(left, -1)
    if tm_count == 4:
        near_two = (None,)
        twos = [lax.ppermute(near, "tm", [(i, (i + 2) % 4) for i in range(4)])]
        far_in = lax.ppermute(far, "tm", [(0, 3), (3, 0)])
        far_shape = (2, three, features)
    else:
        near_two = (-2, 2)
        twos = [shifted(near, 2), shifted(near, -2)]
        far_in = lax.all_gather(far, "tm")
        far_shape = (tm_count, 2, three, features)

    def held(*shape):
        lead = len(shape) - 1
        return pl.BlockSpec(shape[:-1] + (width,), lambda g, i, *_: (0,) * lead + (g,))

    row_spec = pl.BlockSpec((PER_STEP * BLOCK, width), lambda g, i, *_: (i, g))
    pool_rows = rows + 2 * RIM + rows // 4 + 2 * RIM + tm_count * (BLOCK + three) + tm_count * three // 4
    back = 2 * RIM + two
    grads = pl.pallas_call(
        lambda *refs: attend_kernel(tm_count, near_two, *refs),
        grid_spec=pltpu.PrefetchScalarGridSpec(
            num_scalar_prefetch=2,
            grid=(parts, blocks // PER_STEP),
            in_specs=[
                row_spec,
                row_spec,
                held(rows, features),
                held(rows, features),
                held(2, 4, 4, features),
            ]
            + [held(2, pack, features)] * 4
            + [held(2, two + three, features)] * len(twos)
            + [held(*far_shape)],
            out_specs=[
                row_spec,
                row_spec,
                held(2, rows, features),
                held(2, rows // 4, features),
                held(2, two, features),
                held(2, back, features),
                held(2, back, features),
            ]
            + [held(2, two, features)] * len(twos)
            + [held(*far_shape)],
            scratch_shapes=[
                pltpu.VMEM((pool_rows, width), BF16),
                pltpu.VMEM((pool_rows, width), BF16),
                pltpu.VMEM((pool_rows, width), F32),
                pltpu.VMEM((pool_rows, width), F32),
                pltpu.VMEM((width // LANES, tm_count * three, LANES), F32),
                pltpu.VMEM((width // LANES, tm_count * BLOCK, LANES), F32),
            ],
        ),
        out_shape=[
            shape_of(rows, features),
            shape_of(rows, features),
            shape_of(2, rows, features, dtype=F32),
            shape_of(2, rows // 4, features, dtype=F32),
            shape_of(2, two, features, dtype=F32),
            shape_of(2, back, features),
            shape_of(2, back, features),
        ]
        + [shape_of(2, two, features)] * len(twos)
        + [shape_of(*far_shape)],
        compiler_params=params,
        name="attend",
    )(
        position,
        block_links,
        queries,
        out_grad,
        key_vecs,
        value_vecs,
        coarse_taps,
        left,
        right,
        below,
        above,
        *twos,
        far_in,
    )
    attended, grad_query, g_zero, g_one, g_two, to_below, to_above = grads[:7]
    to_twos = grads[7 : 7 + len(twos)]
    to_far = grads[-1]
    from_below = shifted(to_above, 1)
    from_above = shifted(to_below, -1)
    if tm_count == 4:
        from_twos = [lax.ppermute(to_twos[0], "tm", [(i, (i + 2) % 4) for i in range(4)])]
        from_far = lax.ppermute(to_far, "tm", [(0, 3), (3, 0)])
    else:
        from_twos = [shifted(grad, shift) for grad, shift in zip(to_twos, near_two)]
        from_far = lax.psum_scatter(to_far, "tm", scatter_dimension=0)
    grad_key, grad_value = pl.pallas_call(
        lambda *refs: finish_kernel(len(twos), *refs),
        grid=(parts,),
        in_specs=[
            plain(2, rows, features),
            plain(2, rows // 4, features),
            plain(2, two, features),
            taps_spec,
            plain(2, back, features),
            plain(2, back, features),
        ]
        + [plain(2, two, features)] * len(twos)
        + [plain(2, three, features)],
        out_specs=[plain(rows, features), plain(rows, features)],
        out_shape=[shape_of(rows, features), shape_of(rows, features)],
        scratch_shapes=[
            pltpu.VMEM((width // LANES, rows, LANES), F32),
            pltpu.VMEM((width // LANES, rows // 4, LANES), F32),
            pltpu.VMEM((width // LANES, two, LANES), F32),
        ],
        compiler_params=params,
        name="finish",
    )(g_zero, g_one, g_two, coarse_taps, from_below, from_above, *from_twos, from_far)
    return tuple(x[None] for x in (attended, grad_query, grad_key, grad_value))


def solution(mesh):
    spec = P(("groups", "series"), "tm", "head")
    in_specs = (spec, spec, spec, spec, P("tm", None), P(None, None, None, "head"))
    return jax.shard_map(shards, mesh=mesh, in_specs=in_specs, out_specs=(spec,) * 4, check_vma=False)
```

```python
import jax
import jax.numpy as jnp
from jax import lax
from jax.experimental import pallas as pl
from jax.experimental.pallas import tpu as pltpu
from jax.sharding import PartitionSpec as P

HEAD_DIM = 64
BLOCK = 64
RIM = 2 * BLOCK
NEAR = 7 * BLOCK
PER_STEP = 8
VMEM_LIMIT = 56 * 1024 * 1024
F32 = jnp.float32
BF16 = jnp.bfloat16


def dot(a, b, ca, cb):
    return lax.dot_general(a, b, (((ca,), (cb,)), ((), ())), preferred_element_type=F32)


LANES = 128


def widen(scratch, value, at=0):
    for c in range(value.shape[1] // LANES):
        scratch[c, pl.ds(at, value.shape[0]), :] = value[:, c * LANES : (c + 1) * LANES].astype(F32)


def coarse_rows(scratch, count, taps_ref, which, depth):
    parts = []
    for c in range(scratch.shape[0]):
        lanes = slice(c * LANES, (c + 1) * LANES)
        total = None
        for t in range(4):
            part = scratch[c, pl.ds(t, count, stride=4), :] * taps_ref[which, depth, t : t + 1, lanes]
            total = part if total is None else total + part
        parts.append(total)
    return jnp.concatenate(parts, axis=1)


def spread_rows(scratch, coarse, taps_ref, which, depth):
    count = coarse.shape[0]
    parts = []
    for c in range(scratch.shape[0]):
        lanes = slice(c * LANES, (c + 1) * LANES)
        for t in range(4):
            scratch[c, pl.ds(t, count, stride=4), :] = (
                coarse[:, lanes] * taps_ref[which, depth, t : t + 1, lanes]
            )
        parts.append(scratch[c, : 4 * count, :])
    return jnp.concatenate(parts, axis=1)


def when_else(cond, body):
    @pl.when(cond)
    def _():
        body(True)

    @pl.when(jnp.logical_not(cond))
    def _():
        body(False)


def coarsen_kernel(parts, pos_ref, k_ref, v_ref, taps_ref, one_ref, two_ref, far_ref, *rest):
    packs, (wide, mid, low) = rest[: 2 * parts], rest[2 * parts :]
    rows = k_ref.shape[0]
    one, two, three = rows // 4, rows // 16, rows // 64
    even = lax.rem(pos_ref[0], 2) == 0
    for which, own in ((0, k_ref), (1, v_ref)):
        widen(wide, own[...])
        level_one = coarse_rows(wide, one, taps_ref, which, 0).astype(BF16)
        one_ref[which] = level_one
        widen(mid, level_one)
        level_two = coarse_rows(mid, two, taps_ref, which, 1).astype(BF16)
        two_ref[which] = level_two
        widen(low, level_two)
        far_ref[which] = coarse_rows(low, three, taps_ref, which, 2).astype(BF16)
        for n in range(parts):

            @pl.when(pl.program_id(0) == n)
            def _():
                def fill(is_even):
                    for to_next, target in ((is_even, packs[2 * n]), (not is_even, packs[2 * n + 1])):
                        target[which, :RIM] = own[rows - RIM :] if to_next else own[:RIM]
                        target[which, RIM : 2 * RIM] = one_ref[which, one - RIM :] if to_next else one_ref[which, :RIM]
                        target[which, 2 * RIM :] = two_ref[which]

                when_else(even, fill)


def attend_kernel(tm_count, near_two, group_first, *refs):
    (
        pos_ref,
        links_ref,
        q_ref,
        g_ref,
        k_ref,
        v_ref,
        taps_ref,
        one_ref,
        two_ref,
        first_ref,
        second_ref,
    ) = refs[:11]
    rest = refs[11:]
    extra = len(near_two)
    twos, far_ref, rest = rest[:extra], rest[extra], rest[extra + 1 :]
    att_ref, gq_ref, g_zero, g_one, g_two = rest[:5]
    to_twos, to_far, rest = rest[5 : 5 + extra], rest[5 + extra], rest[6 + extra :]
    to_first, to_second, k_pool, v_pool, k_acc, v_acc, three_f32, two_f32, fold = rest
    step = pl.program_id(0)
    last = pl.num_programs(0) - 1
    position = pos_ref[0]
    even = lax.rem(position, 2) == 0
    rows = k_ref.shape[0]
    width = k_ref.shape[1]
    heads = width // HEAD_DIM
    blocks = rows // BLOCK
    one_rows = rows // 4
    base_one = rows + 2 * RIM
    base_two = base_one + one_rows + 2 * RIM
    base_three = base_two + tm_count * BLOCK
    three = rows // 64
    base_four = base_three + tm_count * three
    four_rows = tm_count * three // 4
    upper = tm_count * three + four_rows

    @pl.when(step == 0)
    def _():
        for which, pool, own in ((0, k_pool, k_ref), (1, v_pool, v_ref)):
            pool[RIM : RIM + rows] = own[...]
            pool[base_one + RIM : base_two - RIM] = one_ref[which]

            def place(source, at, owner):
                spot = pl.multiple_of(base_two + owner * BLOCK, BLOCK)
                block = source[which, at : at + BLOCK]
                pool[pl.ds(spot, BLOCK), :] = block
                widen(two_f32, block)
                spot_three = pl.multiple_of(owner * three, three)
                widen(
                    three_f32,
                    coarse_rows(two_f32, three, taps_ref, which, 2).astype(BF16),
                    spot_three,
                )

            if tm_count == 4:

                @pl.when((position == 0) | (position == 3))
                def _():
                    spot = pl.multiple_of((3 - position) * three, three)
                    widen(three_f32, far_ref[which], spot)

            else:
                for owner in range(tm_count):
                    widen(three_f32, far_ref[owner, which], owner * three)
            place(two_ref, 0, position)

            def rims(is_even):
                below, above = (second_ref, first_ref) if is_even else (first_ref, second_ref)
                pool[:RIM] = below[which, :RIM]
                pool[RIM + rows : base_one] = above[which, :RIM]
                pool[base_one : base_one + RIM] = below[which, RIM : 2 * RIM]
                pool[base_two - RIM : base_two] = above[which, RIM : 2 * RIM]

                @pl.when(position > 0)
                def _():
                    place(below, 2 * RIM, position - 1)

                @pl.when(position < tm_count - 1)
                def _():
                    place(above, 2 * RIM, position + 1)

            when_else(even, rims)
            for source, shift in zip(twos, near_two):
                if shift is None:
                    place(source, 0, lax.rem(position + 2, 4))
                else:

                    @pl.when((position + shift >= 0) & (position + shift < tm_count))
                    def _():
                        place(source, 0, position + shift)

            for c in range(width // LANES):
                pool[base_three:base_four, c * LANES : (c + 1) * LANES] = three_f32[c].astype(BF16)
            pool[base_four : base_four + four_rows] = coarse_rows(
                three_f32, four_rows, taps_ref, which, 3
            ).astype(BF16)
        k_acc[...] = jnp.zeros_like(k_acc)
        v_acc[...] = jnp.zeros_like(v_acc)

    first_zero = position * blocks - 2
    first_one = position * (blocks // 4) - 2
    stacked = heads * BLOCK
    row_head = lax.broadcasted_iota(jnp.int32, (stacked, width), 0) // BLOCK
    lane_head = lax.broadcasted_iota(jnp.int32, (stacked, width), 1) // HEAD_DIM
    same = row_head == lane_head

    def diagonal(block):
        wide = jnp.concatenate([block] * heads, axis=0)
        return jnp.where(same, wide, 0.0).astype(BF16)

    low_lanes = lax.broadcasted_iota(jnp.int32, (BLOCK, LANES), 1) < HEAD_DIM

    def folded(product):
        parts = []
        for pair in range(width // LANES):
            span = slice(pair * LANES, (pair + 1) * LANES)
            turned = product[span, span].T
            parts.append(jnp.where(low_lanes, turned[:BLOCK], turned[BLOCK:]))
        return jnp.concatenate(parts, axis=1).astype(BF16)

    def products(unit):
        at = unit * BLOCK
        block = step * PER_STEP + unit
        own = position * blocks + block
        spots = [
            (block + 2) * BLOCK,
            (links_ref[block, 0] - first_zero) * BLOCK,
            (links_ref[block, 1] - first_zero) * BLOCK,
            base_one + (own // 4 - first_one) * BLOCK,
            base_one + (links_ref[block, 2] - first_one) * BLOCK,
            base_two + (own // 16) * BLOCK,
            base_two + links_ref[block, 3] * BLOCK,
        ]
        spots = [pl.multiple_of(spot, BLOCK) for spot in spots]

        def gathered(pool):
            parts = [pool[pl.ds(spot, BLOCK), :] for spot in spots]
            return jnp.concatenate(parts + [pool[base_three : base_three + upper]], axis=0)

        q_diag = diagonal(q_ref[at : at + BLOCK].astype(F32) * 0.125)
        g_diag = diagonal(g_ref[at : at + BLOCK].astype(F32))
        keys = gathered(k_pool)
        values = gathered(v_pool)
        scores = dot(keys, q_diag, 1, 1)
        dprob = dot(values, g_diag, 1, 1)
        return at, spots, q_diag, g_diag, keys, values, scores, dprob

    def softmax(state):
        at, spots, q_diag, g_diag, keys, values, scores, dprob = state
        row_max = jnp.max(scores, axis=0, keepdims=True)
        exponent = jnp.exp(scores - row_max)
        probs = exponent * (1.0 / jnp.sum(exponent, axis=0, keepdims=True))
        probs_b = probs.astype(BF16)
        row_delta = jnp.sum(probs * dprob, axis=0, keepdims=True)
        dscore = (probs * (dprob - row_delta)).astype(BF16)
        return at, spots, q_diag, g_diag, keys, values, probs_b, dscore

    def gradients(state):
        at, spots, q_diag, g_diag, keys, values, probs_b, dscore = state
        att_ref[at : at + BLOCK] = folded(dot(values, probs_b, 0, 0))
        gq_ref[at : at + BLOCK] = folded(dot(keys, dscore, 0, 0) * 0.125)
        grad_k = dot(dscore, q_diag, 1, 0)
        grad_v = dot(probs_b, g_diag, 1, 0)
        for acc, grad in ((k_acc, grad_k), (v_acc, grad_v)):
            for n, spot in enumerate(spots):
                acc[pl.ds(spot, BLOCK), :] += grad[n * BLOCK : (n + 1) * BLOCK]
            acc[base_three : base_three + upper] += grad[NEAR:]

    ahead = products(0)
    behind = None
    for unit in range(PER_STEP):
        now = ahead
        if unit + 1 < PER_STEP:
            ahead = products(unit + 1)
        if behind is not None:
            gradients(behind)
        behind = softmax(now)
    gradients(behind)

    @pl.when(step == last)
    def _():
        for which, acc in ((0, k_acc), (1, v_acc)):
            four = acc[base_four : base_four + four_rows]
            acc[base_three:base_four] += spread_rows(fold, four, taps_ref, which, 3)
            acc[base_two:base_three] += spread_rows(fold, acc[base_three:base_four], taps_ref, which, 2)
            g_zero[which] = acc[RIM : RIM + rows]
            g_one[which] = acc[base_one + RIM : base_two - RIM]

            def slot(owner):
                return acc[pl.ds(pl.multiple_of(base_two + owner * BLOCK, BLOCK), BLOCK), :]

            g_two[which] = slot(position)

            def rims(is_even):
                below, above = (to_second, to_first) if is_even else (to_first, to_second)
                below[which, :RIM] = acc[:RIM].astype(BF16)
                below[which, RIM : 2 * RIM] = acc[base_one : base_one + RIM].astype(BF16)
                below[which, 2 * RIM :] = slot(jnp.maximum(position - 1, 0)).astype(BF16)
                above[which, :RIM] = acc[RIM + rows : base_one].astype(BF16)
                above[which, RIM : 2 * RIM] = acc[base_two - RIM : base_two].astype(BF16)
                above[which, 2 * RIM :] = slot(jnp.minimum(position + 1, tm_count - 1)).astype(BF16)

            when_else(even, rims)
            for target, shift in zip(to_twos, near_two):
                if shift is None:
                    target[which] = slot(lax.rem(position + 2, 4)).astype(BF16)
                else:
                    target[which] = slot(jnp.clip(position + shift, 0, tm_count - 1)).astype(BF16)
            if tm_count == 4:
                spot = pl.multiple_of(base_three + (3 - position) * three, three)
                to_far[which] = acc[pl.ds(spot, three), :].astype(BF16)
            else:
                for owner in range(tm_count):
                    part = acc[base_three + owner * three : base_three + (owner + 1) * three]
                    is_far = (position - owner > 2) | (owner - position > 2)
                    to_far[owner, which] = jnp.where(is_far, part, 0.0).astype(BF16)


def finish_kernel(parts, two_count, pos_ref, g_zero, g_one, g_two, taps_ref, *rest):
    twos, far_ref, rest = rest[:two_count], rest[two_count], rest[two_count + 1 :]
    packs, (gk_ref, gv_ref, zero, one, two) = rest[: 2 * parts], rest[2 * parts :]
    rows = g_zero.shape[1]
    one_rows = rows // 4
    even = lax.rem(pos_ref[0], 2) == 0

    def run(first, second):
        for which, out in ((0, gk_ref), (1, gv_ref)):
            total = g_two[which] + first[which, 2 * RIM :].astype(F32) + second[which, 2 * RIM :].astype(F32)
            for extra in twos:
                total += extra[which].astype(F32)
            total += spread_rows(two, far_ref[which].astype(F32), taps_ref, which, 2)
            ones = spread_rows(one, total, taps_ref, which, 1) + g_one[which]

            def write(is_even):
                below, above = (second, first) if is_even else (first, second)
                parts_one = [ones[:RIM] + below[which, RIM : 2 * RIM].astype(F32)]
                if one_rows > 2 * RIM:
                    parts_one.append(ones[RIM : one_rows - RIM])
                parts_one.append(ones[one_rows - RIM :] + above[which, RIM : 2 * RIM].astype(F32))
                zeros = spread_rows(zero, jnp.concatenate(parts_one, axis=0), taps_ref, which, 0) + g_zero[which]
                out[:RIM] = (zeros[:RIM] + below[which, :RIM].astype(F32)).astype(BF16)
                out[RIM : rows - RIM] = zeros[RIM : rows - RIM].astype(BF16)
                out[rows - RIM :] = (zeros[rows - RIM :] + above[which, :RIM].astype(F32)).astype(BF16)

            when_else(even, write)

    for n in range(parts):

        @pl.when(pl.program_id(0) == n)
        def _():
            run(packs[2 * n], packs[2 * n + 1])


def exchange(first, second):
    count = lax.axis_size("tm")

    def pairs(start):
        low = range(start, count - 1, 2)
        return [(i, i + 1) for i in low] + [(i + 1, i) for i in low]

    return lax.ppermute(first, "tm", pairs(0)), lax.ppermute(second, "tm", pairs(1))


def shifted(x, shift):
    count = lax.axis_size("tm")
    return lax.ppermute(x, "tm", [(i, i + shift) for i in range(count) if 0 <= i + shift < count])


def shards(queries, key_vecs, value_vecs, out_grad, block_links, coarse_taps):
    queries, key_vecs, value_vecs, out_grad = (x[0] for x in (queries, key_vecs, value_vecs, out_grad))
    rows, features = queries.shape
    tm_count = lax.axis_size("tm")
    position = lax.axis_index("tm").astype(jnp.int32).reshape(1)
    width = min(features, 256)
    parts = features // width
    blocks = rows // BLOCK
    one, two, three = rows // 4, rows // 16, rows // 64
    pack = 2 * RIM + two
    pool_rows = rows + 2 * RIM + one + 2 * RIM + tm_count * (BLOCK + three) + tm_count * three // 4
    params = pltpu.CompilerParams(vmem_limit_bytes=VMEM_LIMIT)
    near_two = (None,) if tm_count == 4 else (-2, 2)
    far_lead = (2, three) if tm_count == 4 else (tm_count, 2, three)
    cross = [(i, (i + 2) % 4) for i in range(4)]

    def whole(*shape):
        return pl.BlockSpec(shape, lambda *_: (0,) * len(shape))

    def lanes_of(g, *lead):
        return pl.BlockSpec(lead + (width,), lambda *_: (0,) * len(lead) + (g,))

    def lanes_at(*lead):
        return pl.BlockSpec(lead + (width,), lambda g, *_: (0,) * len(lead) + (g,))

    def shape_of(*shape, dtype=BF16):
        return jax.ShapeDtypeStruct(shape, dtype)

    def wide_scratch(*counts):
        return [pltpu.VMEM((width // LANES, count, LANES), F32) for count in counts]

    level_one, near, far, *packs = pl.pallas_call(
        lambda *refs: coarsen_kernel(parts, *refs),
        grid_spec=pltpu.PrefetchScalarGridSpec(
            num_scalar_prefetch=1,
            grid=(parts,),
            in_specs=[lanes_at(rows), lanes_at(rows), lanes_at(2, 4, 4)],
            out_specs=[lanes_at(2, one), lanes_at(2, two), lanes_at(2, three)]
            + [whole(2, pack, width)] * (2 * parts),
            scratch_shapes=wide_scratch(rows, one, two),
        ),
        out_shape=[shape_of(2, count, features) for count in (one, two, three)]
        + [shape_of(2, pack, width)] * (2 * parts),
        compiler_params=params,
        name="coarsen",
    )(position, key_vecs, value_vecs, coarse_taps)

    def attend(g, one_in, two_in, pair, twos, far_in, earlier):
        row_spec = pl.BlockSpec((PER_STEP * BLOCK, width), lambda i, *_: (i, g))
        count = 11 + len(near_two) + 1
        return pl.pallas_call(
            lambda *refs: attend_kernel(tm_count, near_two, g == 0, *refs[:count], *refs[count + len(earlier) :]),
            grid_spec=pltpu.PrefetchScalarGridSpec(
                num_scalar_prefetch=2,
                grid=(blocks // PER_STEP,),
                in_specs=[
                    row_spec,
                    row_spec,
                    lanes_of(g, rows),
                    lanes_of(g, rows),
                    lanes_of(g, 2, 4, 4),
                    lanes_of(g, 2, one),
                    lanes_of(g, 2, two),
                    whole(2, pack, width),
                    whole(2, pack, width),
                ]
                + [lanes_of(g, 2, two)] * len(near_two)
                + [lanes_of(g, *far_lead)]
                + [pl.BlockSpec(memory_space=pl.ANY)] * len(earlier),
                out_specs=[row_spec, row_spec]
                + [lanes_of(g, 2, count_rows) for count_rows in (rows, one, two)]
                + [lanes_of(g, 2, two)] * len(near_two)
                + [lanes_of(g, *far_lead)]
                + [whole(2, pack, width)] * 2,
                scratch_shapes=[
                    pltpu.VMEM((pool_rows, width), BF16),
                    pltpu.VMEM((pool_rows, width), BF16),
                    pltpu.VMEM((pool_rows, width), F32),
                    pltpu.VMEM((pool_rows, width), F32),
                ]
                + wide_scratch(tm_count * three, BLOCK, tm_count * BLOCK),
            ),
            out_shape=[shape_of(rows, features), shape_of(rows, features)]
            + [shape_of(2, count_rows, features, dtype=F32) for count_rows in (rows, one, two)]
            + [shape_of(2, two, features)] * len(near_two)
            + [shape_of(*far_lead, features)]
            + [shape_of(2, pack, width)] * 2,
            input_output_aliases={count + n: n for n in range(len(earlier))},
            compiler_params=params,
            name="attend",
        )(
            position,
            block_links,
            queries,
            out_grad,
            key_vecs,
            value_vecs,
            coarse_taps,
            one_in,
            two_in,
            *pair,
            *twos,
            far_in,
            *earlier,
        )

    pair = exchange(packs[0], packs[1])
    if tm_count == 4:
        twos = [lax.ppermute(near, "tm", cross)]
        far_in = lax.ppermute(far, "tm", [(0, 3), (3, 0)])
    else:
        twos = [shifted(near, 2), shifted(near, -2)]
        far_in = lax.all_gather(far, "tm")
    shared, returned = [], []
    for g in range(parts):
        if g + 1 < parts:
            pair, twos, far_in, later = lax.optimization_barrier(
                (pair, twos, far_in, tuple(packs[2 * g + 2 : 2 * g + 4]))
            )
            coming = exchange(*later)
        outs = attend(g, level_one, near, pair, twos, far_in, shared)
        shared = list(outs[:-2])
        if g + 1 < parts:
            pair = coming
        returned.append(exchange(*outs[-2:]))
    attended, grad_query, *owns = shared
    to_twos, to_far = owns[3:-1], owns[-1]
    if tm_count == 4:
        from_twos = [lax.ppermute(to_twos[0], "tm", cross)]
        from_far = lax.ppermute(to_far, "tm", [(0, 3), (3, 0)])
    else:
        from_twos = [shifted(grad, shift) for grad, shift in zip(to_twos, near_two)]
        from_far = lax.psum_scatter(to_far, "tm", scatter_dimension=0)
    grad_key, grad_value = pl.pallas_call(
        lambda *refs: finish_kernel(parts, len(near_two), *refs),
        grid_spec=pltpu.PrefetchScalarGridSpec(
            num_scalar_prefetch=1,
            grid=(parts,),
            in_specs=[lanes_at(2, rows), lanes_at(2, one), lanes_at(2, two), lanes_at(2, 4, 4)]
            + [lanes_at(2, two)] * len(near_two)
            + [lanes_at(2, three)]
            + [whole(2, pack, width)] * (2 * parts),
            out_specs=[lanes_at(rows)] * 2,
            scratch_shapes=wide_scratch(rows, one, two),
        ),
        out_shape=[shape_of(rows, features)] * 2,
        compiler_params=params,
        name="finish",
    )(position, *owns[:3], coarse_taps, *from_twos, from_far, *[x for both in returned for x in both])
    return tuple(x[None] for x in (attended, grad_query, grad_key, grad_value))


def solution(mesh):
    spec = P(("groups", "series"), "tm", "head")
    in_specs = (spec, spec, spec, spec, P("tm", None), P(None, None, None, "head"))
    return jax.shard_map(shards, mesh=mesh, in_specs=in_specs, out_specs=(spec,) * 4, check_vma=False)
```

```python
import jax
import jax.numpy as jnp
from jax import lax
from jax.experimental import pallas as pl
from jax.experimental.pallas import tpu as pltpu
from jax.sharding import PartitionSpec as P

HEAD_DIM = 64
BLOCK = 64
RIM = 2 * BLOCK
NEAR = 7 * BLOCK
PER_STEP = 8
VMEM_LIMIT = 56 * 1024 * 1024
F32 = jnp.float32
BF16 = jnp.bfloat16


def dot(a, b, ca, cb):
    return lax.dot_general(a, b, (((ca,), (cb,)), ((), ())), preferred_element_type=F32)


LANES = 128


def widen(scratch, value, at=0):
    for c in range(value.shape[1] // LANES):
        scratch[c, pl.ds(at, value.shape[0]), :] = value[:, c * LANES : (c + 1) * LANES].astype(F32)


def coarse_rows(scratch, count, taps_ref, which, depth):
    parts = []
    for c in range(scratch.shape[0]):
        lanes = slice(c * LANES, (c + 1) * LANES)
        total = None
        for t in range(4):
            part = scratch[c, pl.ds(t, count, stride=4), :] * taps_ref[which, depth, t : t + 1, lanes]
            total = part if total is None else total + part
        parts.append(total)
    return jnp.concatenate(parts, axis=1)


def spread_rows(scratch, coarse, taps_ref, which, depth):
    count = coarse.shape[0]
    parts = []
    for c in range(scratch.shape[0]):
        lanes = slice(c * LANES, (c + 1) * LANES)
        for t in range(4):
            scratch[c, pl.ds(t, count, stride=4), :] = (
                coarse[:, lanes] * taps_ref[which, depth, t : t + 1, lanes]
            )
        parts.append(scratch[c, : 4 * count, :])
    return jnp.concatenate(parts, axis=1)


def when_else(cond, body):
    @pl.when(cond)
    def _():
        body(True)

    @pl.when(jnp.logical_not(cond))
    def _():
        body(False)


def coarsen_kernel(parts, pos_ref, k_ref, v_ref, taps_ref, one_ref, far_ref, *rest):
    packs, (wide, mid, low) = rest[: 3 * parts], rest[3 * parts :]
    rows = k_ref.shape[0]
    one, two, three = rows // 4, rows // 16, rows // 64
    even = lax.rem(pos_ref[0], 2) == 0
    for which, own in ((0, k_ref), (1, v_ref)):
        widen(wide, own[...])
        level_one = coarse_rows(wide, one, taps_ref, which, 0).astype(BF16)
        one_ref[which] = level_one
        widen(mid, level_one)
        level_two = coarse_rows(mid, two, taps_ref, which, 1).astype(BF16)
        widen(low, level_two)
        far_ref[which] = coarse_rows(low, three, taps_ref, which, 2).astype(BF16)
        for n in range(parts):

            @pl.when(pl.program_id(0) == n)
            def _():
                packs[3 * n + 2][which] = level_two

                def fill(is_even):
                    for to_next, target in ((is_even, packs[3 * n]), (not is_even, packs[3 * n + 1])):
                        target[which, :RIM] = own[rows - RIM :] if to_next else own[:RIM]
                        target[which, RIM : 2 * RIM] = one_ref[which, one - RIM :] if to_next else one_ref[which, :RIM]
                        target[which, 2 * RIM :] = level_two

                when_else(even, fill)


def attend_kernel(tm_count, near_two, group, *refs):
    (
        pos_ref,
        links_ref,
        q_ref,
        g_ref,
        k_ref,
        v_ref,
        taps_ref,
        one_ref,
        two_ref,
        first_ref,
        second_ref,
    ) = refs[:11]
    rest = refs[11:]
    extra = len(near_two)
    twos, far_ref, rest = rest[:extra], rest[extra], rest[extra + 1 :]
    att_ref, gq_ref, g_zero, g_one, g_two = rest[:5]
    to_far, to_twos, rest = rest[5], rest[6 : 6 + extra], rest[6 + extra :]
    to_first, to_second, k_pool, v_pool, k_acc, v_acc, three_f32, two_f32, fold, sems = rest
    step = pl.program_id(0)
    last = pl.num_programs(0) - 1
    position = pos_ref[0]
    even = lax.rem(position, 2) == 0
    rows = k_ref.shape[0]
    width = q_ref.shape[1]
    heads = width // HEAD_DIM
    blocks = rows // BLOCK
    one_rows = rows // 4
    base_one = rows + 2 * RIM
    base_two = base_one + one_rows + 2 * RIM
    base_three = base_two + tm_count * BLOCK
    three = rows // 64
    base_four = base_three + tm_count * three
    four_rows = tm_count * three // 4
    upper = tm_count * three + four_rows

    @pl.when(step == 0)
    def _():
        lanes = pl.ds(group * width, width)
        copies = []

        def copy(source, target, when=None):
            copies.append((pltpu.make_async_copy(source, target, sems.at[len(copies)]), when))

        def block_of(pool, owner):
            return pool.at[pl.ds(pl.multiple_of(base_two + owner * BLOCK, BLOCK), BLOCK)]

        for which, pool, own in ((0, k_pool, k_ref), (1, v_pool, v_ref)):
            copy(own.at[:, lanes], pool.at[pl.ds(RIM, rows)])
            copy(one_ref.at[group, which], pool.at[pl.ds(base_one + RIM, one_rows)])
            copy(two_ref.at[which], block_of(pool, position))
            for pair_ref, after in ((first_ref, even), (second_ref, jnp.logical_not(even))):
                for side, exists in ((after, position < tm_count - 1), (jnp.logical_not(after), position > 0)):
                    up = exists is not None and side is after
                    zero_at, one_at, owner = (
                        (RIM + rows, base_two - RIM, position + 1) if up else (0, base_one, position - 1)
                    )
                    use = jnp.logical_and(side, exists)
                    copy(pair_ref.at[which, pl.ds(0, RIM)], pool.at[pl.ds(zero_at, RIM)], use)
                    copy(pair_ref.at[which, pl.ds(RIM, RIM)], pool.at[pl.ds(one_at, RIM)], use)
                    copy(pair_ref.at[which, pl.ds(2 * RIM, BLOCK)], block_of(pool, owner), use)
            for source, shift in zip(twos, near_two):
                if shift is None:
                    copy(source.at[which], block_of(pool, lax.rem(position + 2, 4)))
                else:
                    use = (position + shift >= 0) & (position + shift < tm_count)
                    copy(source.at[which], block_of(pool, position + shift), use)

        def run(method):
            for made, use in copies:
                if use is None:
                    getattr(made, method)()
                else:

                    @pl.when(use)
                    def _():
                        getattr(made, method)()

        run("start")
        k_acc[...] = jnp.zeros_like(k_acc)
        v_acc[...] = jnp.zeros_like(v_acc)
        run("wait")
        for which, pool in ((0, k_pool), (1, v_pool)):
            if tm_count == 4:
                widen(two_f32, pool[base_two:base_three])
                widen(three_f32, coarse_rows(two_f32, tm_count * three, taps_ref, which, 2).astype(BF16))

                @pl.when((position == 0) | (position == 3))
                def _():
                    spot = pl.multiple_of((3 - position) * three, three)
                    widen(three_f32, far_ref[which], spot)

            else:
                for owner in range(tm_count):
                    widen(three_f32, far_ref[owner, which], owner * three)
            for c in range(width // LANES):
                pool[base_three:base_four, c * LANES : (c + 1) * LANES] = three_f32[c].astype(BF16)
            pool[base_four : base_four + four_rows] = coarse_rows(
                three_f32, four_rows, taps_ref, which, 3
            ).astype(BF16)

    first_zero = position * blocks - 2
    first_one = position * (blocks // 4) - 2
    stacked = heads * BLOCK
    row_head = lax.broadcasted_iota(jnp.int32, (stacked, width), 0) // BLOCK
    lane_head = lax.broadcasted_iota(jnp.int32, (stacked, width), 1) // HEAD_DIM
    same = row_head == lane_head

    def diagonal(block):
        wide = jnp.concatenate([block] * heads, axis=0)
        return jnp.where(same, wide, 0.0).astype(BF16)

    low_lanes = lax.broadcasted_iota(jnp.int32, (BLOCK, LANES), 1) < HEAD_DIM

    def folded(product):
        parts = []
        for pair in range(width // LANES):
            span = slice(pair * LANES, (pair + 1) * LANES)
            turned = product[span, span].T
            parts.append(jnp.where(low_lanes, turned[:BLOCK], turned[BLOCK:]))
        return jnp.concatenate(parts, axis=1).astype(BF16)

    def products(unit):
        at = unit * BLOCK
        block = step * PER_STEP + unit
        own = position * blocks + block
        spots = [
            (block + 2) * BLOCK,
            (links_ref[0, block] - first_zero) * BLOCK,
            (links_ref[1, block] - first_zero) * BLOCK,
            base_one + (own // 4 - first_one) * BLOCK,
            base_one + (links_ref[2, block] - first_one) * BLOCK,
            base_two + (own // 16) * BLOCK,
            base_two + links_ref[3, block] * BLOCK,
        ]
        spots = [pl.multiple_of(spot, BLOCK) for spot in spots]

        def gathered(pool):
            parts = [pool[pl.ds(spot, BLOCK), :] for spot in spots]
            return jnp.concatenate(parts + [pool[base_three : base_three + upper]], axis=0)

        q_diag = diagonal(q_ref[at : at + BLOCK].astype(F32) * 0.125)
        g_diag = diagonal(g_ref[at : at + BLOCK].astype(F32))
        keys = gathered(k_pool)
        values = gathered(v_pool)
        scores = dot(keys, q_diag, 1, 1)
        dprob = dot(values, g_diag, 1, 1)
        return at, spots, q_diag, g_diag, keys, values, scores, dprob

    def softmax(state):
        at, spots, q_diag, g_diag, keys, values, scores, dprob = state
        row_max = jnp.max(scores, axis=0, keepdims=True)
        exponent = jnp.exp(scores - row_max)
        probs = exponent * (1.0 / jnp.sum(exponent, axis=0, keepdims=True))
        probs_b = probs.astype(BF16)
        row_delta = jnp.sum(probs * dprob, axis=0, keepdims=True)
        dscore = (probs * (dprob - row_delta)).astype(BF16)
        return at, spots, q_diag, g_diag, keys, values, probs_b, dscore

    def gradients(state):
        at, spots, q_diag, g_diag, keys, values, probs_b, dscore = state
        att_ref[at : at + BLOCK] = folded(dot(values, probs_b, 0, 0))
        gq_ref[at : at + BLOCK] = folded(dot(keys, dscore, 0, 0) * 0.125)
        grad_k = dot(dscore, q_diag, 1, 0)
        grad_v = dot(probs_b, g_diag, 1, 0)
        for acc, grad in ((k_acc, grad_k), (v_acc, grad_v)):
            for n, spot in enumerate(spots):
                acc[pl.ds(spot, BLOCK), :] += grad[n * BLOCK : (n + 1) * BLOCK]
            acc[base_three : base_three + upper] += grad[NEAR:]

    ahead = products(0)
    behind = None
    for unit in range(PER_STEP):
        now = ahead
        if unit + 1 < PER_STEP:
            ahead = products(unit + 1)
        if behind is not None:
            gradients(behind)
        behind = softmax(now)
    gradients(behind)

    @pl.when(step == last)
    def _():
        for which, acc in ((0, k_acc), (1, v_acc)):
            four = acc[base_four : base_four + four_rows]
            acc[base_three:base_four] += spread_rows(fold, four, taps_ref, which, 3)
            acc[base_two:base_three] += spread_rows(fold, acc[base_three:base_four], taps_ref, which, 2)
            g_zero[which] = acc[RIM : RIM + rows].astype(BF16)
            g_one[which] = acc[base_one + RIM : base_two - RIM]

            def slot(owner):
                return acc[pl.ds(pl.multiple_of(base_two + owner * BLOCK, BLOCK), BLOCK), :]

            g_two[which] = slot(position)

            def rims(is_even):
                below, above = (to_second, to_first) if is_even else (to_first, to_second)
                below[which, :RIM] = acc[:RIM].astype(BF16)
                below[which, RIM : 2 * RIM] = acc[base_one : base_one + RIM].astype(BF16)
                below[which, 2 * RIM :] = slot(jnp.maximum(position - 1, 0)).astype(BF16)
                above[which, :RIM] = acc[RIM + rows : base_one].astype(BF16)
                above[which, RIM : 2 * RIM] = acc[base_two - RIM : base_two].astype(BF16)
                above[which, 2 * RIM :] = slot(jnp.minimum(position + 1, tm_count - 1)).astype(BF16)

            when_else(even, rims)
            for target, shift in zip(to_twos, near_two):
                if shift is None:
                    target[which] = slot(lax.rem(position + 2, 4)).astype(BF16)
                else:
                    target[which] = slot(jnp.clip(position + shift, 0, tm_count - 1)).astype(BF16)
            if tm_count == 4:
                spot = pl.multiple_of(base_three + (3 - position) * three, three)
                to_far[which] = acc[pl.ds(spot, three), :].astype(BF16)
            else:
                for owner in range(tm_count):
                    part = acc[base_three + owner * three : base_three + (owner + 1) * three]
                    is_far = (position - owner > 2) | (owner - position > 2)
                    to_far[owner, which] = jnp.where(is_far, part, 0.0).astype(BF16)


def finish_kernel(parts, two_count, pos_ref, g_zero, g_one, g_two, taps_ref, *rest):
    per = 2 + two_count
    far_ref, packs = rest[0], rest[1 : 1 + per * parts]
    gk_ref, gv_ref, zero, one, two, far_two, total_zero, rim_in, two_in = rest[1 + per * parts :]
    rows, two_rows = g_zero.shape[1], g_two.shape[1]
    group, chunk = pl.program_id(0), pl.program_id(1)
    below_second = lax.rem(pos_ref[0], 2) == 0
    use_second = below_second == (chunk == 0)
    two_at = pl.ds(pl.multiple_of(2 * RIM + chunk * two_rows, two_rows), two_rows)
    near_at = pl.ds(pl.multiple_of(chunk * two_rows, two_rows), two_rows)
    for n in range(parts):

        @pl.when(group == n)
        def _():
            twos, first, second = packs[per * n : per * n + two_count], *packs[per * n + two_count : per * n + per]

            @pl.when(use_second)
            def _():
                rim_in[...] = second[:, : 2 * RIM]

            @pl.when(jnp.logical_not(use_second))
            def _():
                rim_in[...] = first[:, : 2 * RIM]

            total = first[:, two_at, :].astype(F32) + second[:, two_at, :].astype(F32)
            for extra in twos:
                total += extra[:, near_at, :].astype(F32)
            two_in[...] = total

    rim_at = pl.ds(pl.multiple_of(chunk * (rows - RIM), RIM), RIM)
    for which, out in ((0, gk_ref), (1, gv_ref)):
        total = g_two[which] + two_in[which]
        far_two[...] = spread_rows(two, far_ref[which].astype(F32), taps_ref, which, 2)
        total += far_two[pl.ds(pl.multiple_of(chunk * two_rows, two_rows), two_rows), :]
        ones = spread_rows(one, total, taps_ref, which, 1) + g_one[which] + rim_in[which, RIM:].astype(F32)
        total_zero[...] = spread_rows(zero, ones, taps_ref, which, 0) + g_zero[which].astype(F32)
        total_zero[rim_at, :] += rim_in[which, :RIM].astype(F32)
        out[...] = total_zero[...].astype(BF16)


def exchange(near, first, second):
    count = lax.axis_size("tm")

    def pairs(start):
        low = range(start, count - 1, 2)
        return [(i, i + 1) for i in low] + [(i + 1, i) for i in low]

    second = lax.ppermute(second, "tm", pairs(1))
    if count == 4:
        near = [lax.ppermute(near[0], "tm", [(i, (i + 2) % 4) for i in range(4)])]
    else:
        near = [shifted(x, shift) for x, shift in zip(near, (-2, 2))]
    return near, [lax.ppermute(first, "tm", pairs(0)), second]


def shifted(x, shift):
    count = lax.axis_size("tm")
    return lax.ppermute(x, "tm", [(i, i + shift) for i in range(count) if 0 <= i + shift < count])


def shards(queries, key_vecs, value_vecs, out_grad, block_links, coarse_taps):
    queries, key_vecs, value_vecs, out_grad = (x[0] for x in (queries, key_vecs, value_vecs, out_grad))
    rows, features = queries.shape
    tm_count = lax.axis_size("tm")
    position = lax.axis_index("tm").astype(jnp.int32).reshape(1)
    width = min(features, 256)
    parts = features // width
    blocks = rows // BLOCK
    one, two, three = rows // 4, rows // 16, rows // 64
    pack = 2 * RIM + two
    pool_rows = rows + 2 * RIM + one + 2 * RIM + tm_count * (BLOCK + three) + tm_count * three // 4
    params = pltpu.CompilerParams(vmem_limit_bytes=VMEM_LIMIT)
    near_two = (None,) if tm_count == 4 else (-2, 2)
    far_shape = (parts, 2, three, width) if tm_count == 4 else (tm_count, parts, 2, three, width)

    def whole(*shape):
        return pl.BlockSpec(shape, lambda *_: (0,) * len(shape))

    def lanes_of(g, *lead):
        return pl.BlockSpec(lead + (width,), lambda *_: (0,) * len(lead) + (g,))

    def grouped(g, *lead):
        return pl.BlockSpec((None,) + lead + (width,), lambda *_: (g,) + (0,) * (len(lead) + 1))

    def grouped_at(*lead):
        return pl.BlockSpec((None,) + lead + (width,), lambda g, *_: (g,) + (0,) * (len(lead) + 1))

    def far_spec(g):
        if tm_count == 4:
            return grouped(g, 2, three)
        return pl.BlockSpec((tm_count, None, 2, three, width), lambda *_: (0, g, 0, 0, 0))

    def lanes_at(*lead):
        return pl.BlockSpec(lead + (width,), lambda g, *_: (0,) * len(lead) + (g,))

    in_place = pl.BlockSpec(memory_space=pl.ANY)

    def shape_of(*shape, dtype=BF16):
        return jax.ShapeDtypeStruct(shape, dtype)

    def wide_scratch(*counts):
        return [pltpu.VMEM((width // LANES, count, LANES), F32) for count in counts]

    level_one, far, *packs = pl.pallas_call(
        lambda *refs: coarsen_kernel(parts, *refs),
        grid_spec=pltpu.PrefetchScalarGridSpec(
            num_scalar_prefetch=1,
            grid=(parts,),
            in_specs=[lanes_at(rows), lanes_at(rows), lanes_at(2, 4, 4)],
            out_specs=[grouped_at(2, one), grouped_at(2, three)]
            + [whole(2, count, width) for count in (pack, pack, two)] * parts,
            scratch_shapes=wide_scratch(rows, one, two),
        ),
        out_shape=[shape_of(parts, 2, count, width) for count in (one, three)]
        + [shape_of(2, count, width) for count in (pack, pack, two)] * parts,
        compiler_params=params,
        name="coarsen",
    )(position, key_vecs, value_vecs, coarse_taps)

    def attend(g, one_in, two_in, pair, twos, far_in, earlier):
        row_spec = pl.BlockSpec((PER_STEP * BLOCK, width), lambda i, *_: (i, g))
        count = 11 + len(near_two) + 1
        pairs_done = rows * (NEAR + tm_count * (three + three // 4)) * (width // HEAD_DIM)
        cost = pl.CostEstimate(
            flops=24 * pairs_done * width, transcendentals=pairs_done, bytes_accessed=16 * rows * width
        )
        return pl.pallas_call(
            lambda *refs: attend_kernel(tm_count, near_two, g, *refs[:count], *refs[count + len(earlier) :]),
            grid_spec=pltpu.PrefetchScalarGridSpec(
                num_scalar_prefetch=2,
                grid=(blocks // PER_STEP,),
                in_specs=[
                    row_spec,
                    row_spec,
                    in_place,
                    in_place,
                    lanes_of(g, 2, 4, 4),
                ]
                + [in_place] * (4 + len(near_two))
                + [far_spec(g)]
                + [in_place] * len(earlier),
                out_specs=[row_spec, row_spec]
                + [grouped(g, 2, count_rows) for count_rows in (rows, one, two)]
                + [far_spec(g)]
                + [whole(2, two, width)] * len(near_two)
                + [whole(2, pack, width)] * 2,
                scratch_shapes=[
                    pltpu.VMEM((pool_rows, width), BF16),
                    pltpu.VMEM((pool_rows, width), BF16),
                    pltpu.VMEM((pool_rows, width), F32),
                    pltpu.VMEM((pool_rows, width), F32),
                ]
                + wide_scratch(tm_count * three, tm_count * BLOCK, tm_count * BLOCK)
                + [pltpu.SemaphoreType.DMA((2 * (15 + len(near_two)),))],
            ),
            out_shape=[shape_of(rows, features), shape_of(rows, features)]
            + [shape_of(parts, 2, rows, width)]
            + [shape_of(parts, 2, count_rows, width, dtype=F32) for count_rows in (one, two)]
            + [shape_of(*far_shape)]
            + [shape_of(2, two, width)] * len(near_two)
            + [shape_of(2, pack, width)] * 2,
            input_output_aliases={count + n: n for n in range(len(earlier))},
            compiler_params=params,
            cost_estimate=cost,
            name="attend",
        )(
            position,
            block_links.T,
            queries,
            out_grad,
            key_vecs,
            value_vecs,
            coarse_taps,
            one_in,
            two_in,
            *pair,
            *twos,
            far_in,
            *earlier,
        )

    def exchange_of(n):
        first, second, near = packs[3 * n : 3 * n + 3]
        return exchange([near] * len(near_two), first, second)

    twos, pair = exchange_of(0)
    if tm_count == 4:
        far_in = lax.ppermute(far, "tm", [(0, 3), (3, 0)])
    else:
        twos = twos[::-1]
        far_in = lax.all_gather(far, "tm")
    shared, returned = [], []
    for g in range(parts):
        if g + 1 < parts:
            pair, twos, far_in, later = lax.optimization_barrier(
                (pair, twos, far_in, tuple(packs[3 * g + 3 : 3 * g + 6]))
            )
            coming = exchange([later[2]] * len(near_two), later[0], later[1])
        outs = attend(g, level_one, packs[3 * g + 2], pair, twos, far_in, shared)
        shared = list(outs[:6])
        if g + 1 < parts:
            twos, pair = coming
        leaving = list(outs[6:])
        if g > 0:
            leaving, returned[-1] = lax.optimization_barrier((leaving, returned[-1]))
        returned.append(exchange(leaving[:-2], leaving[-2], leaving[-1]))
    attended, grad_query, *owns, to_far = shared
    if tm_count == 4:
        from_far = lax.ppermute(to_far, "tm", [(0, 3), (3, 0)])
    else:
        from_far = lax.psum_scatter(to_far, "tm", scatter_dimension=0)
    chunks = one // RIM

    def chunk_of(count):
        return pl.BlockSpec((None, 2, count // chunks, width), lambda g, c, *_: (g, 0, c, 0))

    grad_key, grad_value = pl.pallas_call(
        lambda *refs: finish_kernel(parts, len(near_two), *refs),
        grid_spec=pltpu.PrefetchScalarGridSpec(
            num_scalar_prefetch=1,
            grid=(parts, chunks),
            in_specs=[chunk_of(rows), chunk_of(one), chunk_of(two), lanes_at(2, 4, 4)]
            + [grouped_at(2, three)]
            + ([whole(2, two, width)] * len(near_two) + [whole(2, pack, width)] * 2) * parts,
            out_specs=[pl.BlockSpec((rows // chunks, width), lambda g, c, *_: (c, g))] * 2,
            scratch_shapes=wide_scratch(rows // chunks, RIM, two)
            + [
                pltpu.VMEM((two, width), F32),
                pltpu.VMEM((rows // chunks, width), F32),
                pltpu.VMEM((2, 2 * RIM, width), BF16),
                pltpu.VMEM((2, two // chunks, width), F32),
            ],
        ),
        out_shape=[shape_of(rows, features)] * 2,
        compiler_params=params,
        name="finish",
    )(position, *owns, coarse_taps, from_far, *[x for twos, pair in returned for x in (*twos, *pair)])
    return tuple(x[None] for x in (attended, grad_query, grad_key, grad_value))


def solution(mesh):
    spec = P(("groups", "series"), "tm", "head")
    in_specs = (spec, spec, spec, spec, P("tm", None), P(None, None, None, "head"))
    return jax.shard_map(shards, mesh=mesh, in_specs=in_specs, out_specs=(spec,) * 4, check_vma=False)
```

```python
import jax
import jax.numpy as jnp
from jax import lax
from jax.experimental import pallas as pl
from jax.experimental.pallas import tpu as pltpu
from jax.sharding import PartitionSpec as P

HEAD_DIM = 64
BLOCK = 64
RIM = 2 * BLOCK
NEAR = 7 * BLOCK
PER_STEP = 8
VMEM_LIMIT = 56 * 1024 * 1024
F32 = jnp.float32
BF16 = jnp.bfloat16


def dot(a, b, ca, cb):
    return lax.dot_general(a, b, (((ca,), (cb,)), ((), ())), preferred_element_type=F32)


LANES = 128


def widen(scratch, value, at=0):
    for c in range(value.shape[1] // LANES):
        scratch[c, pl.ds(at, value.shape[0]), :] = value[:, c * LANES : (c + 1) * LANES].astype(F32)


def coarse_rows(scratch, count, taps_ref, which, depth):
    parts = []
    for c in range(scratch.shape[0]):
        lanes = slice(c * LANES, (c + 1) * LANES)
        total = None
        for t in range(4):
            part = scratch[c, pl.ds(t, count, stride=4), :] * taps_ref[which, depth, t : t + 1, lanes]
            total = part if total is None else total + part
        parts.append(total)
    return jnp.concatenate(parts, axis=1)


def spread_rows(scratch, coarse, taps_ref, which, depth):
    count = coarse.shape[0]
    parts = []
    for c in range(scratch.shape[0]):
        lanes = slice(c * LANES, (c + 1) * LANES)
        for t in range(4):
            scratch[c, pl.ds(t, count, stride=4), :] = (
                coarse[:, lanes] * taps_ref[which, depth, t : t + 1, lanes]
            )
        parts.append(scratch[c, : 4 * count, :])
    return jnp.concatenate(parts, axis=1)


def when_else(cond, body):
    @pl.when(cond)
    def _():
        body(True)

    @pl.when(jnp.logical_not(cond))
    def _():
        body(False)


def coarsen_kernel(parts, pos_ref, k_ref, v_ref, taps_ref, one_ref, far_ref, *rest):
    packs, (wide, mid, low) = rest[: 3 * parts], rest[3 * parts :]
    rows = k_ref.shape[0]
    one, two, three = rows // 4, rows // 16, rows // 64
    even = lax.rem(pos_ref[0], 2) == 0
    for which, own in ((0, k_ref), (1, v_ref)):
        widen(wide, own[...])
        level_one = coarse_rows(wide, one, taps_ref, which, 0).astype(BF16)
        one_ref[which] = level_one
        widen(mid, level_one)
        level_two = coarse_rows(mid, two, taps_ref, which, 1).astype(BF16)
        widen(low, level_two)
        far_ref[which] = coarse_rows(low, three, taps_ref, which, 2).astype(BF16)
        for n in range(parts):

            @pl.when(pl.program_id(0) == n)
            def _():
                packs[3 * n + 2][which] = level_two

                def fill(is_even):
                    for to_next, target in ((is_even, packs[3 * n]), (not is_even, packs[3 * n + 1])):
                        target[which, :RIM] = own[rows - RIM :] if to_next else own[:RIM]
                        target[which, RIM : 2 * RIM] = one_ref[which, one - RIM :] if to_next else one_ref[which, :RIM]
                        target[which, 2 * RIM :] = level_two

                when_else(even, fill)


def attend_kernel(tm_count, near_two, group, *refs):
    (
        pos_ref,
        links_ref,
        q_in,
        g_in,
        k_ref,
        v_ref,
        taps_in,
        one_ref,
        two_ref,
        first_ref,
        second_ref,
    ) = refs[:11]
    rest = refs[11:]
    extra = len(near_two)
    twos, far_in, rest = rest[:extra], rest[extra], rest[extra + 1 :]
    att_ref, gq_ref, g_zero, g_one, g_two = rest[:5]
    to_far, to_twos, rest = rest[5], rest[6 : 6 + extra], rest[6 + extra :]
    to_first, to_second, k_pool, v_pool, k_acc, v_acc, three_f32, two_f32, fold, q_ref, g_ref, taps_ref, far_ref, sems = rest
    step = pl.program_id(0)
    last = pl.num_programs(0) - 1
    position = pos_ref[0]
    even = lax.rem(position, 2) == 0
    rows = k_ref.shape[0]
    width = q_ref.shape[1]
    heads = width // HEAD_DIM
    blocks = rows // BLOCK
    one_rows = rows // 4
    base_one = rows + 2 * RIM
    base_two = base_one + one_rows + 2 * RIM
    base_three = base_two + tm_count * BLOCK
    three = rows // 64
    base_four = base_three + tm_count * three
    four_rows = tm_count * three // 4
    upper = tm_count * three + four_rows

    @pl.when(step == 0)
    def _():
        lanes = pl.ds(group * width, width)
        copies = []

        def copy(source, target, when=None):
            copies.append((pltpu.make_async_copy(source, target, sems.at[len(copies)]), when))

        def block_of(pool, owner):
            return pool.at[pl.ds(pl.multiple_of(base_two + owner * BLOCK, BLOCK), BLOCK)]

        copy(q_in.at[:, lanes], q_ref)
        copy(g_in.at[:, lanes], g_ref)
        copy(taps_in.at[:, :, :, lanes], taps_ref)
        copy(far_in.at[group] if tm_count == 4 else far_in.at[:, group], far_ref)
        for which, pool, own in ((0, k_pool, k_ref), (1, v_pool, v_ref)):
            copy(own.at[:, lanes], pool.at[pl.ds(RIM, rows)])
            copy(one_ref.at[group, which], pool.at[pl.ds(base_one + RIM, one_rows)])
            copy(two_ref.at[which], block_of(pool, position))
            for pair_ref, after in ((first_ref, even), (second_ref, jnp.logical_not(even))):
                for side, exists in ((after, position < tm_count - 1), (jnp.logical_not(after), position > 0)):
                    up = exists is not None and side is after
                    zero_at, one_at, owner = (
                        (RIM + rows, base_two - RIM, position + 1) if up else (0, base_one, position - 1)
                    )
                    use = jnp.logical_and(side, exists)
                    copy(pair_ref.at[which, pl.ds(0, RIM)], pool.at[pl.ds(zero_at, RIM)], use)
                    copy(pair_ref.at[which, pl.ds(RIM, RIM)], pool.at[pl.ds(one_at, RIM)], use)
                    copy(pair_ref.at[which, pl.ds(2 * RIM, BLOCK)], block_of(pool, owner), use)
            for source, shift in zip(twos, near_two):
                if shift is None:
                    copy(source.at[which], block_of(pool, lax.rem(position + 2, 4)))
                else:
                    use = (position + shift >= 0) & (position + shift < tm_count)
                    copy(source.at[which], block_of(pool, position + shift), use)

        def run(method):
            for made, use in copies:
                if use is None:
                    getattr(made, method)()
                else:

                    @pl.when(use)
                    def _():
                        getattr(made, method)()

        run("start")
        k_acc[...] = jnp.zeros_like(k_acc)
        v_acc[...] = jnp.zeros_like(v_acc)
        run("wait")
        for which, pool in ((0, k_pool), (1, v_pool)):
            if tm_count == 4:
                widen(two_f32, pool[base_two:base_three])
                widen(three_f32, coarse_rows(two_f32, tm_count * three, taps_ref, which, 2).astype(BF16))

                @pl.when((position == 0) | (position == 3))
                def _():
                    spot = pl.multiple_of((3 - position) * three, three)
                    widen(three_f32, far_ref[which], spot)

            else:
                for owner in range(tm_count):
                    widen(three_f32, far_ref[owner, which], owner * three)
            for c in range(width // LANES):
                pool[base_three:base_four, c * LANES : (c + 1) * LANES] = three_f32[c].astype(BF16)
            pool[base_four : base_four + four_rows] = coarse_rows(
                three_f32, four_rows, taps_ref, which, 3
            ).astype(BF16)

    first_zero = position * blocks - 2
    first_one = position * (blocks // 4) - 2
    stacked = heads * BLOCK
    row_head = lax.broadcasted_iota(jnp.int32, (stacked, width), 0) // BLOCK
    lane_head = lax.broadcasted_iota(jnp.int32, (stacked, width), 1) // HEAD_DIM
    same = row_head == lane_head

    def diagonal(block):
        wide = jnp.concatenate([block] * heads, axis=0)
        return jnp.where(same, wide, 0.0).astype(BF16)

    low_lanes = lax.broadcasted_iota(jnp.int32, (BLOCK, LANES), 1) < HEAD_DIM

    def folded(product):
        parts = []
        for pair in range(width // LANES):
            span = slice(pair * LANES, (pair + 1) * LANES)
            turned = product[span, span].T
            parts.append(jnp.where(low_lanes, turned[:BLOCK], turned[BLOCK:]))
        return jnp.concatenate(parts, axis=1).astype(BF16)

    def products(unit):
        at = unit * BLOCK
        block = step * PER_STEP + unit
        own = position * blocks + block
        spots = [
            (block + 2) * BLOCK,
            (links_ref[0, block] - first_zero) * BLOCK,
            (links_ref[1, block] - first_zero) * BLOCK,
            base_one + (own // 4 - first_one) * BLOCK,
            base_one + (links_ref[2, block] - first_one) * BLOCK,
            base_two + (own // 16) * BLOCK,
            base_two + links_ref[3, block] * BLOCK,
        ]
        spots = [pl.multiple_of(spot, BLOCK) for spot in spots]

        def gathered(pool):
            parts = [pool[pl.ds(spot, BLOCK), :] for spot in spots]
            return jnp.concatenate(parts + [pool[base_three : base_three + upper]], axis=0)

        q_diag = diagonal(q_ref[pl.ds(pl.multiple_of(block * BLOCK, BLOCK), BLOCK), :].astype(F32) * 0.125)
        g_diag = diagonal(g_ref[pl.ds(pl.multiple_of(block * BLOCK, BLOCK), BLOCK), :].astype(F32))
        keys = gathered(k_pool)
        values = gathered(v_pool)
        scores = dot(keys, q_diag, 1, 1)
        dprob = dot(values, g_diag, 1, 1)
        return at, spots, q_diag, g_diag, keys, values, scores, dprob

    def softmax(state):
        at, spots, q_diag, g_diag, keys, values, scores, dprob = state
        row_max = jnp.max(scores, axis=0, keepdims=True)
        exponent = jnp.exp(scores - row_max)
        probs = exponent * (1.0 / jnp.sum(exponent, axis=0, keepdims=True))
        probs_b = probs.astype(BF16)
        row_delta = jnp.sum(probs * dprob, axis=0, keepdims=True)
        dscore = (probs * (dprob - row_delta)).astype(BF16)
        return at, spots, q_diag, g_diag, keys, values, probs_b, dscore

    def gradients(state):
        at, spots, q_diag, g_diag, keys, values, probs_b, dscore = state
        att_ref[at : at + BLOCK] = folded(dot(values, probs_b, 0, 0))
        gq_ref[at : at + BLOCK] = folded(dot(keys, dscore, 0, 0) * 0.125)
        grad_k = dot(dscore, q_diag, 1, 0)
        grad_v = dot(probs_b, g_diag, 1, 0)
        for acc, grad in ((k_acc, grad_k), (v_acc, grad_v)):
            for n, spot in enumerate(spots):
                acc[pl.ds(spot, BLOCK), :] += grad[n * BLOCK : (n + 1) * BLOCK]
            acc[base_three : base_three + upper] += grad[NEAR:]

    ahead = products(0)
    behind = None
    for unit in range(PER_STEP):
        now = ahead
        if unit + 1 < PER_STEP:
            ahead = products(unit + 1)
        if behind is not None:
            gradients(behind)
        behind = softmax(now)
    gradients(behind)

    @pl.when(step == last)
    def _():
        for which, acc in ((0, k_acc), (1, v_acc)):
            four = acc[base_four : base_four + four_rows]
            acc[base_three:base_four] += spread_rows(fold, four, taps_ref, which, 3)
            acc[base_two:base_three] += spread_rows(fold, acc[base_three:base_four], taps_ref, which, 2)
            g_zero[which] = acc[RIM : RIM + rows].astype(BF16)
            g_one[which] = acc[base_one + RIM : base_two - RIM]

            def slot(owner):
                return acc[pl.ds(pl.multiple_of(base_two + owner * BLOCK, BLOCK), BLOCK), :]

            g_two[which] = slot(position)

            def rims(is_even):
                below, above = (to_second, to_first) if is_even else (to_first, to_second)
                below[which, :RIM] = acc[:RIM].astype(BF16)
                below[which, RIM : 2 * RIM] = acc[base_one : base_one + RIM].astype(BF16)
                below[which, 2 * RIM :] = slot(jnp.maximum(position - 1, 0)).astype(BF16)
                above[which, :RIM] = acc[RIM + rows : base_one].astype(BF16)
                above[which, RIM : 2 * RIM] = acc[base_two - RIM : base_two].astype(BF16)
                above[which, 2 * RIM :] = slot(jnp.minimum(position + 1, tm_count - 1)).astype(BF16)

            when_else(even, rims)
            for target, shift in zip(to_twos, near_two):
                if shift is None:
                    target[which] = slot(lax.rem(position + 2, 4)).astype(BF16)
                else:
                    target[which] = slot(jnp.clip(position + shift, 0, tm_count - 1)).astype(BF16)
            if tm_count == 4:
                spot = pl.multiple_of(base_three + (3 - position) * three, three)
                to_far[which] = acc[pl.ds(spot, three), :].astype(BF16)
            else:
                for owner in range(tm_count):
                    part = acc[base_three + owner * three : base_three + (owner + 1) * three]
                    is_far = (position - owner > 2) | (owner - position > 2)
                    to_far[owner, which] = jnp.where(is_far, part, 0.0).astype(BF16)


def finish_kernel(two_count, pos_ref, g_zero, g_one, g_two, taps_ref, *rest):
    twos, (first, second, far_ref) = rest[:two_count], rest[two_count : two_count + 3]
    gk_ref, gv_ref, zero, one, two, far_two, rim_in = rest[two_count + 3 :]
    rows, two_rows = g_zero.shape[1], g_two.shape[1]
    chunk = pl.program_id(0)
    below_second = lax.rem(pos_ref[0], 2) == 0

    def take(use_second):
        rim_in[...] = (second if use_second else first)[:, : 2 * RIM]

    when_else(below_second == (chunk == 0), take)
    two_at = pl.ds(pl.multiple_of(2 * RIM + chunk * two_rows, two_rows), two_rows)
    near_at = pl.ds(pl.multiple_of(chunk * two_rows, two_rows), two_rows)
    rim_at = pl.ds(pl.multiple_of(chunk * (rows - RIM), RIM), RIM)
    for which, out in ((0, gk_ref), (1, gv_ref)):
        total = g_two[which] + first[which, two_at, :].astype(F32) + second[which, two_at, :].astype(F32)
        for extra in twos:
            total += extra[which, near_at, :].astype(F32)
        far_two[...] = spread_rows(two, far_ref[which].astype(F32), taps_ref, which, 2)
        total += far_two[near_at, :]
        ones = spread_rows(one, total, taps_ref, which, 1) + g_one[which] + rim_in[which, RIM:].astype(F32)
        out[...] = (spread_rows(zero, ones, taps_ref, which, 0) + g_zero[which].astype(F32)).astype(BF16)
        rim_rows = jnp.concatenate([zero[c, rim_at, :] for c in range(zero.shape[0])], axis=1)
        rim_rows += g_zero[which, rim_at, :].astype(F32) + rim_in[which, :RIM].astype(F32)
        out[rim_at, :] = rim_rows.astype(BF16)


def exchange(near, first, second):
    count = lax.axis_size("tm")

    def pairs(start):
        low = range(start, count - 1, 2)
        return [(i, i + 1) for i in low] + [(i + 1, i) for i in low]

    second = lax.ppermute(second, "tm", pairs(1))
    if count == 4:
        near = [lax.ppermute(near[0], "tm", [(i, (i + 2) % 4) for i in range(4)])]
    else:
        near = [shifted(x, shift) for x, shift in zip(near, (-2, 2))]
    return near, [lax.ppermute(first, "tm", pairs(0)), second]


def shifted(x, shift):
    count = lax.axis_size("tm")
    return lax.ppermute(x, "tm", [(i, i + shift) for i in range(count) if 0 <= i + shift < count])


def shards(queries, key_vecs, value_vecs, out_grad, block_links, coarse_taps):
    queries, key_vecs, value_vecs, out_grad = (x[0] for x in (queries, key_vecs, value_vecs, out_grad))
    rows, features = queries.shape
    tm_count = lax.axis_size("tm")
    position = lax.axis_index("tm").astype(jnp.int32).reshape(1)
    width = min(features, 256)
    parts = features // width
    blocks = rows // BLOCK
    one, two, three = rows // 4, rows // 16, rows // 64
    pack = 2 * RIM + two
    pool_rows = rows + 2 * RIM + one + 2 * RIM + tm_count * (BLOCK + three) + tm_count * three // 4
    params = pltpu.CompilerParams(vmem_limit_bytes=VMEM_LIMIT)
    near_two = (None,) if tm_count == 4 else (-2, 2)

    def whole(*shape):
        return pl.BlockSpec(shape, lambda *_: (0,) * len(shape))

    def lanes_of(g, *lead):
        return pl.BlockSpec(lead + (width,), lambda *_: (0,) * len(lead) + (g,))

    def grouped(g, *lead):
        return pl.BlockSpec((None,) + lead + (width,), lambda *_: (g,) + (0,) * (len(lead) + 1))

    def grouped_at(*lead):
        return pl.BlockSpec((None,) + lead + (width,), lambda g, *_: (g,) + (0,) * (len(lead) + 1))

    def far_back():
        return (2, three, width) if tm_count == 4 else (tm_count, 2, three, width)

    def lanes_at(*lead):
        return pl.BlockSpec(lead + (width,), lambda g, *_: (0,) * len(lead) + (g,))

    in_place = pl.BlockSpec(memory_space=pl.ANY)

    def shape_of(*shape, dtype=BF16):
        return jax.ShapeDtypeStruct(shape, dtype)

    def wide_scratch(*counts):
        return [pltpu.VMEM((width // LANES, count, LANES), F32) for count in counts]

    level_one, far, *packs = pl.pallas_call(
        lambda *refs: coarsen_kernel(parts, *refs),
        grid_spec=pltpu.PrefetchScalarGridSpec(
            num_scalar_prefetch=1,
            grid=(parts,),
            in_specs=[lanes_at(rows), lanes_at(rows), lanes_at(2, 4, 4)],
            out_specs=[grouped_at(2, one), grouped_at(2, three)]
            + [whole(2, count, width) for count in (pack, pack, two)] * parts,
            scratch_shapes=wide_scratch(rows, one, two),
        ),
        out_shape=[shape_of(parts, 2, count, width) for count in (one, three)]
        + [shape_of(2, count, width) for count in (pack, pack, two)] * parts,
        compiler_params=params,
        name="coarsen",
    )(position, key_vecs, value_vecs, coarse_taps)

    def attend(g, one_in, two_in, pair, twos, far_in, earlier):
        row_spec = pl.BlockSpec((PER_STEP * BLOCK, width), lambda i, *_: (i, g))
        count = 11 + len(near_two) + 1
        pairs_done = rows * (NEAR + tm_count * (three + three // 4)) * (width // HEAD_DIM)
        cost = pl.CostEstimate(
            flops=24 * pairs_done * width, transcendentals=pairs_done, bytes_accessed=16 * rows * width
        )
        return pl.pallas_call(
            lambda *refs: attend_kernel(tm_count, near_two, g, *refs[:count], *refs[count + len(earlier) :]),
            grid_spec=pltpu.PrefetchScalarGridSpec(
                num_scalar_prefetch=2,
                grid=(blocks // PER_STEP,),
                in_specs=[in_place] * (count - 2 + len(earlier)),
                out_specs=[row_spec, row_spec]
                + [grouped(g, 2, count_rows) for count_rows in (rows, one, two)]
                + [whole(*far_back())]
                + [whole(2, two, width)] * len(near_two)
                + [whole(2, pack, width)] * 2,
                scratch_shapes=[
                    pltpu.VMEM((pool_rows, width), BF16),
                    pltpu.VMEM((pool_rows, width), BF16),
                    pltpu.VMEM((pool_rows, width), F32),
                    pltpu.VMEM((pool_rows, width), F32),
                ]
                + wide_scratch(tm_count * three, tm_count * BLOCK, tm_count * BLOCK)
                + [
                    pltpu.VMEM((rows, width), BF16),
                    pltpu.VMEM((rows, width), BF16),
                    pltpu.VMEM((2, 4, 4, width), F32),
                    pltpu.VMEM(far_back(), BF16),
                    pltpu.SemaphoreType.DMA((4 + 2 * (15 + len(near_two)),)),
                ],
            ),
            out_shape=[shape_of(rows, features), shape_of(rows, features)]
            + [shape_of(parts, 2, rows, width)]
            + [shape_of(parts, 2, count_rows, width, dtype=F32) for count_rows in (one, two)]
            + [shape_of(*far_back())]
            + [shape_of(2, two, width)] * len(near_two)
            + [shape_of(2, pack, width)] * 2,
            input_output_aliases={count + n: n for n in range(len(earlier))},
            compiler_params=params,
            cost_estimate=cost,
            name="attend",
        )(
            position,
            block_links.T,
            queries,
            out_grad,
            key_vecs,
            value_vecs,
            coarse_taps,
            one_in,
            two_in,
            *pair,
            *twos,
            far_in,
            *earlier,
        )

    def exchange_of(n):
        first, second, near = packs[3 * n : 3 * n + 3]
        return exchange([near] * len(near_two), first, second)

    twos, pair = exchange_of(0)
    if tm_count == 4:
        far_in = lax.ppermute(far, "tm", [(0, 3), (3, 0)])
    else:
        twos = twos[::-1]
        far_in = lax.all_gather(far, "tm")
    shared, returned = [], []
    for g in range(parts):
        if g + 1 < parts:
            pair, twos, far_in, later = lax.optimization_barrier(
                (pair, twos, far_in, tuple(packs[3 * g + 3 : 3 * g + 6]))
            )
            coming = exchange([later[2]] * len(near_two), later[0], later[1])
        outs = attend(g, level_one, packs[3 * g + 2], pair, twos, far_in, shared)
        shared = list(outs[:5])
        if g + 1 < parts:
            twos, pair = coming
        leaving = list(outs[5:])
        if g > 0:
            leaving, returned[-1] = lax.optimization_barrier((leaving, returned[-1]))
        near_in, pair_in = exchange(leaving[1:-2], leaving[-2], leaving[-1])
        if tm_count == 4:
            from_far = lax.ppermute(leaving[0], "tm", [(0, 3), (3, 0)])
        else:
            from_far = lax.psum_scatter(leaving[0], "tm", scatter_dimension=0)
        returned.append([*near_in, *pair_in, from_far])
    attended, grad_query, *owns = shared
    chunks = one // RIM

    def chunk_of(g, count):
        return pl.BlockSpec((None, 2, count // chunks, width), lambda c, *_: (g, 0, c, 0))

    def finish(g, earlier):
        count = 8 + len(near_two)
        return pl.pallas_call(
            lambda *refs: finish_kernel(len(near_two), *refs[:count], *refs[count + len(earlier) :]),
            grid_spec=pltpu.PrefetchScalarGridSpec(
                num_scalar_prefetch=1,
                grid=(chunks,),
                in_specs=[chunk_of(g, rows), chunk_of(g, one), chunk_of(g, two), lanes_of(g, 2, 4, 4)]
                + [whole(2, two, width)] * len(near_two)
                + [whole(2, pack, width)] * 2
                + [whole(2, three, width)]
                + [in_place] * len(earlier),
                out_specs=[pl.BlockSpec((rows // chunks, width), lambda c, *_: (c, g))] * 2,
                scratch_shapes=wide_scratch(rows // chunks, RIM, two)
                + [pltpu.VMEM((two, width), F32), pltpu.VMEM((2, 2 * RIM, width), BF16)],
            ),
            out_shape=[shape_of(rows, features)] * 2,
            input_output_aliases={count + n: n for n in range(len(earlier))},
            compiler_params=params,
            name="finish",
        )(position, *owns, coarse_taps, *returned[g], *earlier)

    grads = []
    for g in range(parts):
        grads = list(finish(g, grads))
    grad_key, grad_value = grads
    return tuple(x[None] for x in (attended, grad_query, grad_key, grad_value))


def solution(mesh):
    spec = P(("groups", "series"), "tm", "head")
    in_specs = (spec, spec, spec, spec, P("tm", None), P(None, None, None, "head"))
    return jax.shard_map(shards, mesh=mesh, in_specs=in_specs, out_specs=(spec,) * 4, check_vma=False)
```

```python
import jax
import jax.numpy as jnp
from jax import lax
from jax.experimental import pallas as pl
from jax.experimental.pallas import tpu as pltpu
from jax.sharding import PartitionSpec as P

HEAD_DIM = 64
BLOCK = 64
RIM = 2 * BLOCK
NEAR = 7 * BLOCK
PER_STEP = 16
VMEM_LIMIT = 56 * 1024 * 1024
F32 = jnp.float32
BF16 = jnp.bfloat16


def dot(a, b, ca, cb):
    return lax.dot_general(a, b, (((ca,), (cb,)), ((), ())), preferred_element_type=F32)


LANES = 128


def widen(scratch, value, at=0):
    for c in range(value.shape[1] // LANES):
        scratch[c, pl.ds(at, value.shape[0]), :] = value[:, c * LANES : (c + 1) * LANES].astype(F32)


def coarse_rows(scratch, count, taps_ref, which, depth):
    parts = []
    for c in range(scratch.shape[0]):
        lanes = slice(c * LANES, (c + 1) * LANES)
        total = None
        for t in range(4):
            part = scratch[c, pl.ds(t, count, stride=4), :] * taps_ref[which, depth, t : t + 1, lanes]
            total = part if total is None else total + part
        parts.append(total)
    return jnp.concatenate(parts, axis=1)


def spread_rows(scratch, coarse, taps_ref, which, depth):
    count = coarse.shape[0]
    parts = []
    for c in range(scratch.shape[0]):
        lanes = slice(c * LANES, (c + 1) * LANES)
        for t in range(4):
            scratch[c, pl.ds(t, count, stride=4), :] = (
                coarse[:, lanes] * taps_ref[which, depth, t : t + 1, lanes]
            )
        parts.append(scratch[c, : 4 * count, :])
    return jnp.concatenate(parts, axis=1)


def when_else(cond, body):
    @pl.when(cond)
    def _():
        body(True)

    @pl.when(jnp.logical_not(cond))
    def _():
        body(False)


def coarsen_kernel(parts, pos_ref, k_ref, v_ref, taps_ref, one_ref, far_ref, *rest):
    packs, (wide, mid, low) = rest[: 3 * parts], rest[3 * parts :]
    rows = k_ref.shape[0]
    one, two, three = rows // 4, rows // 16, rows // 64
    even = lax.rem(pos_ref[0], 2) == 0
    for which, own in ((0, k_ref), (1, v_ref)):
        widen(wide, own[...])
        level_one = coarse_rows(wide, one, taps_ref, which, 0).astype(BF16)
        one_ref[which] = level_one
        widen(mid, level_one)
        level_two = coarse_rows(mid, two, taps_ref, which, 1).astype(BF16)
        widen(low, level_two)
        far_ref[which] = coarse_rows(low, three, taps_ref, which, 2).astype(BF16)
        for n in range(parts):

            @pl.when(pl.program_id(0) == n)
            def _():
                packs[3 * n + 2][which] = level_two

                def fill(is_even):
                    for to_next, target in ((is_even, packs[3 * n]), (not is_even, packs[3 * n + 1])):
                        target[which, :RIM] = own[rows - RIM :] if to_next else own[:RIM]
                        target[which, RIM : 2 * RIM] = one_ref[which, one - RIM :] if to_next else one_ref[which, :RIM]
                        target[which, 2 * RIM :] = level_two

                when_else(even, fill)


def attend_kernel(tm_count, near_two, group, *refs):
    (
        pos_ref,
        links_ref,
        q_in,
        g_in,
        k_ref,
        v_ref,
        taps_in,
        one_ref,
        two_ref,
        first_ref,
        second_ref,
    ) = refs[:11]
    rest = refs[11:]
    extra = len(near_two)
    twos, far_in, rest = rest[:extra], rest[extra], rest[extra + 1 :]
    att_ref, gq_ref, g_zero, g_one, g_two = rest[:5]
    to_far, to_twos, rest = rest[5], rest[6 : 6 + extra], rest[6 + extra :]
    to_first, to_second, k_pool, v_pool, k_acc, v_acc, three_f32, two_f32, fold, q_ref, g_ref, taps_ref, far_ref, sems = rest
    step = pl.program_id(0)
    last = pl.num_programs(0) - 1
    position = pos_ref[0]
    even = lax.rem(position, 2) == 0
    rows = k_ref.shape[0]
    width = q_ref.shape[1]
    heads = width // HEAD_DIM
    blocks = rows // BLOCK
    one_rows = rows // 4
    base_one = rows + 2 * RIM
    base_two = base_one + one_rows + 2 * RIM
    base_three = base_two + tm_count * BLOCK
    three = rows // 64
    base_four = base_three + tm_count * three
    four_rows = tm_count * three // 4
    upper = tm_count * three + four_rows

    @pl.when(step == 0)
    def _():
        lanes = pl.ds(group * width, width)
        copies = []

        def copy(source, target, when=None):
            copies.append((pltpu.make_async_copy(source, target, sems.at[len(copies)]), when))

        def block_of(pool, owner):
            return pool.at[pl.ds(pl.multiple_of(base_two + owner * BLOCK, BLOCK), BLOCK)]

        copy(q_in.at[:, lanes], q_ref)
        copy(g_in.at[:, lanes], g_ref)
        copy(taps_in.at[:, :, :, lanes], taps_ref)
        copy(far_in.at[group] if tm_count == 4 else far_in.at[:, group], far_ref)
        for which, pool, own in ((0, k_pool, k_ref), (1, v_pool, v_ref)):
            copy(own.at[:, lanes], pool.at[pl.ds(RIM, rows)])
            copy(one_ref.at[group, which], pool.at[pl.ds(base_one + RIM, one_rows)])
            copy(two_ref.at[which], block_of(pool, position))
            for pair_ref, after in ((first_ref, even), (second_ref, jnp.logical_not(even))):
                for side, exists in ((after, position < tm_count - 1), (jnp.logical_not(after), position > 0)):
                    up = exists is not None and side is after
                    zero_at, one_at, owner = (
                        (RIM + rows, base_two - RIM, position + 1) if up else (0, base_one, position - 1)
                    )
                    use = jnp.logical_and(side, exists)
                    copy(pair_ref.at[which, pl.ds(0, RIM)], pool.at[pl.ds(zero_at, RIM)], use)
                    copy(pair_ref.at[which, pl.ds(RIM, RIM)], pool.at[pl.ds(one_at, RIM)], use)
                    copy(pair_ref.at[which, pl.ds(2 * RIM, BLOCK)], block_of(pool, owner), use)
            for source, shift in zip(twos, near_two):
                if shift is None:
                    copy(source.at[which], block_of(pool, lax.rem(position + 2, 4)))
                else:
                    use = (position + shift >= 0) & (position + shift < tm_count)
                    copy(source.at[which], block_of(pool, position + shift), use)

        def run(method):
            for made, use in copies:
                if use is None:
                    getattr(made, method)()
                else:

                    @pl.when(use)
                    def _():
                        getattr(made, method)()

        run("start")
        k_acc[...] = jnp.zeros_like(k_acc)
        v_acc[...] = jnp.zeros_like(v_acc)
        run("wait")
        for which, pool in ((0, k_pool), (1, v_pool)):
            if tm_count == 4:
                widen(two_f32, pool[base_two:base_three])
                widen(three_f32, coarse_rows(two_f32, tm_count * three, taps_ref, which, 2).astype(BF16))

                @pl.when((position == 0) | (position == 3))
                def _():
                    spot = pl.multiple_of((3 - position) * three, three)
                    widen(three_f32, far_ref[which], spot)

            else:
                for owner in range(tm_count):
                    widen(three_f32, far_ref[owner, which], owner * three)
            for c in range(width // LANES):
                pool[base_three:base_four, c * LANES : (c + 1) * LANES] = three_f32[c].astype(BF16)
            pool[base_four : base_four + four_rows] = coarse_rows(
                three_f32, four_rows, taps_ref, which, 3
            ).astype(BF16)

    first_zero = position * blocks - 2
    first_one = position * (blocks // 4) - 2
    stacked = heads * BLOCK
    row_head = lax.broadcasted_iota(jnp.int32, (stacked, width), 0) // BLOCK
    lane_head = lax.broadcasted_iota(jnp.int32, (stacked, width), 1) // HEAD_DIM
    same = row_head == lane_head

    def diagonal(block):
        wide = jnp.concatenate([block] * heads, axis=0)
        return jnp.where(same, wide, 0.0).astype(BF16)

    low_lanes = lax.broadcasted_iota(jnp.int32, (BLOCK, LANES), 1) < HEAD_DIM

    def folded(product):
        parts = []
        for pair in range(width // LANES):
            span = slice(pair * LANES, (pair + 1) * LANES)
            turned = product[span, span].T
            parts.append(jnp.where(low_lanes, turned[:BLOCK], turned[BLOCK:]))
        return jnp.concatenate(parts, axis=1).astype(BF16)

    def products(unit):
        at = unit * BLOCK
        block = step * PER_STEP + unit
        own = position * blocks + block
        spots = [
            (block + 2) * BLOCK,
            (links_ref[0, block] - first_zero) * BLOCK,
            (links_ref[1, block] - first_zero) * BLOCK,
            base_one + (own // 4 - first_one) * BLOCK,
            base_one + (links_ref[2, block] - first_one) * BLOCK,
            base_two + (own // 16) * BLOCK,
            base_two + links_ref[3, block] * BLOCK,
        ]
        spots = [pl.multiple_of(spot, BLOCK) for spot in spots]

        def gathered(pool):
            parts = [pool[pl.ds(spot, BLOCK), :] for spot in spots]
            return jnp.concatenate(parts + [pool[base_three : base_three + upper]], axis=0)

        q_diag = diagonal(q_ref[pl.ds(pl.multiple_of(block * BLOCK, BLOCK), BLOCK), :].astype(F32) * 0.125)
        g_diag = diagonal(g_ref[pl.ds(pl.multiple_of(block * BLOCK, BLOCK), BLOCK), :].astype(F32))
        keys = gathered(k_pool)
        values = gathered(v_pool)
        scores = dot(keys, q_diag, 1, 1)
        dprob = dot(values, g_diag, 1, 1)
        return at, spots, q_diag, g_diag, keys, values, scores, dprob

    def softmax(state):
        at, spots, q_diag, g_diag, keys, values, scores, dprob = state
        row_max = jnp.max(scores, axis=0, keepdims=True)
        exponent = jnp.exp(scores - row_max)
        probs = exponent * (1.0 / jnp.sum(exponent, axis=0, keepdims=True))
        probs_b = probs.astype(BF16)
        row_delta = jnp.sum(probs * dprob, axis=0, keepdims=True)
        dscore = (probs * (dprob - row_delta)).astype(BF16)
        return at, spots, q_diag, g_diag, keys, values, probs_b, dscore

    def gradients(state):
        at, spots, q_diag, g_diag, keys, values, probs_b, dscore = state
        att_ref[at : at + BLOCK] = folded(dot(values, probs_b, 0, 0))
        gq_ref[at : at + BLOCK] = folded(dot(keys, dscore, 0, 0) * 0.125)
        grad_k = dot(dscore, q_diag, 1, 0)
        grad_v = dot(probs_b, g_diag, 1, 0)
        for acc, grad in ((k_acc, grad_k), (v_acc, grad_v)):
            for n, spot in enumerate(spots):
                acc[pl.ds(spot, BLOCK), :] += grad[n * BLOCK : (n + 1) * BLOCK]
            acc[base_three : base_three + upper] += grad[NEAR:]

    ahead = products(0)
    behind = None
    for unit in range(PER_STEP):
        now = ahead
        if unit + 1 < PER_STEP:
            ahead = products(unit + 1)
        if behind is not None:
            gradients(behind)
        behind = softmax(now)
    gradients(behind)

    @pl.when(step == last)
    def _():
        for which, acc in ((0, k_acc), (1, v_acc)):
            four = acc[base_four : base_four + four_rows]
            acc[base_three:base_four] += spread_rows(fold, four, taps_ref, which, 3)
            acc[base_two:base_three] += spread_rows(fold, acc[base_three:base_four], taps_ref, which, 2)
            g_zero[which] = acc[RIM : RIM + rows].astype(BF16)
            g_one[which] = acc[base_one + RIM : base_two - RIM]

            def slot(owner):
                return acc[pl.ds(pl.multiple_of(base_two + owner * BLOCK, BLOCK), BLOCK), :]

            g_two[which] = slot(position)

            def rims(is_even):
                below, above = (to_second, to_first) if is_even else (to_first, to_second)
                below[which, :RIM] = acc[:RIM].astype(BF16)
                below[which, RIM : 2 * RIM] = acc[base_one : base_one + RIM].astype(BF16)
                below[which, 2 * RIM :] = slot(jnp.maximum(position - 1, 0)).astype(BF16)
                above[which, :RIM] = acc[RIM + rows : base_one].astype(BF16)
                above[which, RIM : 2 * RIM] = acc[base_two - RIM : base_two].astype(BF16)
                above[which, 2 * RIM :] = slot(jnp.minimum(position + 1, tm_count - 1)).astype(BF16)

            when_else(even, rims)
            for target, shift in zip(to_twos, near_two):
                if shift is None:
                    target[which] = slot(lax.rem(position + 2, 4)).astype(BF16)
                else:
                    target[which] = slot(jnp.clip(position + shift, 0, tm_count - 1)).astype(BF16)
            if tm_count == 4:
                spot = pl.multiple_of(base_three + (3 - position) * three, three)
                to_far[which] = acc[pl.ds(spot, three), :].astype(BF16)
            else:
                for owner in range(tm_count):
                    part = acc[base_three + owner * three : base_three + (owner + 1) * three]
                    is_far = (position - owner > 2) | (owner - position > 2)
                    to_far[owner, which] = jnp.where(is_far, part, 0.0).astype(BF16)


def finish_kernel(two_count, pos_ref, g_zero, g_one, g_two, taps_ref, *rest):
    twos, (first, second, far_ref) = rest[:two_count], rest[two_count : two_count + 3]
    gk_ref, gv_ref, zero, one, two, far_two, rim_in = rest[two_count + 3 :]
    rows, two_rows = g_zero.shape[1], g_two.shape[1]
    chunk = pl.program_id(0)
    below_second = lax.rem(pos_ref[0], 2) == 0

    def take(use_second):
        rim_in[...] = (second if use_second else first)[:, : 2 * RIM]

    when_else(below_second == (chunk == 0), take)
    two_at = pl.ds(pl.multiple_of(2 * RIM + chunk * two_rows, two_rows), two_rows)
    near_at = pl.ds(pl.multiple_of(chunk * two_rows, two_rows), two_rows)
    rim_at = pl.ds(pl.multiple_of(chunk * (rows - RIM), RIM), RIM)
    for which, out in ((0, gk_ref), (1, gv_ref)):
        total = g_two[which] + first[which, two_at, :].astype(F32) + second[which, two_at, :].astype(F32)
        for extra in twos:
            total += extra[which, near_at, :].astype(F32)
        far_two[...] = spread_rows(two, far_ref[which].astype(F32), taps_ref, which, 2)
        total += far_two[near_at, :]
        ones = spread_rows(one, total, taps_ref, which, 1) + g_one[which] + rim_in[which, RIM:].astype(F32)
        out[...] = (spread_rows(zero, ones, taps_ref, which, 0) + g_zero[which].astype(F32)).astype(BF16)
        rim_rows = jnp.concatenate([zero[c, rim_at, :] for c in range(zero.shape[0])], axis=1)
        rim_rows += g_zero[which, rim_at, :].astype(F32) + rim_in[which, :RIM].astype(F32)
        out[rim_at, :] = rim_rows.astype(BF16)


def exchange(near, first, second):
    count = lax.axis_size("tm")

    def pairs(start):
        low = range(start, count - 1, 2)
        return [(i, i + 1) for i in low] + [(i + 1, i) for i in low]

    second = lax.ppermute(second, "tm", pairs(1))
    if count == 4:
        near = [lax.ppermute(near[0], "tm", [(i, (i + 2) % 4) for i in range(4)])]
    else:
        near = [shifted(x, shift) for x, shift in zip(near, (-2, 2))]
    return near, [lax.ppermute(first, "tm", pairs(0)), second]


def shifted(x, shift):
    count = lax.axis_size("tm")
    return lax.ppermute(x, "tm", [(i, i + shift) for i in range(count) if 0 <= i + shift < count])


def shards(queries, key_vecs, value_vecs, out_grad, block_links, coarse_taps):
    queries, key_vecs, value_vecs, out_grad = (x[0] for x in (queries, key_vecs, value_vecs, out_grad))
    rows, features = queries.shape
    tm_count = lax.axis_size("tm")
    position = lax.axis_index("tm").astype(jnp.int32).reshape(1)
    width = min(features, 256)
    parts = features // width
    blocks = rows // BLOCK
    one, two, three = rows // 4, rows // 16, rows // 64
    pack = 2 * RIM + two
    pool_rows = rows + 2 * RIM + one + 2 * RIM + tm_count * (BLOCK + three) + tm_count * three // 4
    params = pltpu.CompilerParams(vmem_limit_bytes=VMEM_LIMIT)
    near_two = (None,) if tm_count == 4 else (-2, 2)

    def whole(*shape):
        return pl.BlockSpec(shape, lambda *_: (0,) * len(shape))

    def lanes_of(g, *lead):
        return pl.BlockSpec(lead + (width,), lambda *_: (0,) * len(lead) + (g,))

    def grouped(g, *lead):
        return pl.BlockSpec((None,) + lead + (width,), lambda *_: (g,) + (0,) * (len(lead) + 1))

    def grouped_at(*lead):
        return pl.BlockSpec((None,) + lead + (width,), lambda g, *_: (g,) + (0,) * (len(lead) + 1))

    def far_back():
        return (2, three, width) if tm_count == 4 else (tm_count, 2, three, width)

    def lanes_at(*lead):
        return pl.BlockSpec(lead + (width,), lambda g, *_: (0,) * len(lead) + (g,))

    in_place = pl.BlockSpec(memory_space=pl.ANY)

    def shape_of(*shape, dtype=BF16):
        return jax.ShapeDtypeStruct(shape, dtype)

    def wide_scratch(*counts):
        return [pltpu.VMEM((width // LANES, count, LANES), F32) for count in counts]

    level_one, far, *packs = pl.pallas_call(
        lambda *refs: coarsen_kernel(parts, *refs),
        grid_spec=pltpu.PrefetchScalarGridSpec(
            num_scalar_prefetch=1,
            grid=(parts,),
            in_specs=[lanes_at(rows), lanes_at(rows), lanes_at(2, 4, 4)],
            out_specs=[grouped_at(2, one), grouped_at(2, three)]
            + [whole(2, count, width) for count in (pack, pack, two)] * parts,
            scratch_shapes=wide_scratch(rows, one, two),
        ),
        out_shape=[shape_of(parts, 2, count, width) for count in (one, three)]
        + [shape_of(2, count, width) for count in (pack, pack, two)] * parts,
        compiler_params=params,
        name="coarsen",
    )(position, key_vecs, value_vecs, coarse_taps)

    def attend(g, one_in, two_in, pair, twos, far_in, earlier):
        row_spec = pl.BlockSpec((PER_STEP * BLOCK, width), lambda i, *_: (i, g))
        count = 11 + len(near_two) + 1
        pairs_done = rows * (NEAR + tm_count * (three + three // 4)) * (width // HEAD_DIM)
        cost = pl.CostEstimate(
            flops=24 * pairs_done * width, transcendentals=pairs_done, bytes_accessed=16 * rows * width
        )
        return pl.pallas_call(
            lambda *refs: attend_kernel(tm_count, near_two, g, *refs[:count], *refs[count + len(earlier) :]),
            grid_spec=pltpu.PrefetchScalarGridSpec(
                num_scalar_prefetch=2,
                grid=(blocks // PER_STEP,),
                in_specs=[in_place] * (count - 2 + len(earlier)),
                out_specs=[row_spec, row_spec]
                + [grouped(g, 2, count_rows) for count_rows in (rows, one, two)]
                + [whole(*far_back())]
                + [whole(2, two, width)] * len(near_two)
                + [whole(2, pack, width)] * 2,
                scratch_shapes=[
                    pltpu.VMEM((pool_rows, width), BF16),
                    pltpu.VMEM((pool_rows, width), BF16),
                    pltpu.VMEM((pool_rows, width), F32),
                    pltpu.VMEM((pool_rows, width), F32),
                ]
                + wide_scratch(tm_count * three, tm_count * BLOCK, tm_count * BLOCK)
                + [
                    pltpu.VMEM((rows, width), BF16),
                    pltpu.VMEM((rows, width), BF16),
                    pltpu.VMEM((2, 4, 4, width), F32),
                    pltpu.VMEM(far_back(), BF16),
                    pltpu.SemaphoreType.DMA((4 + 2 * (15 + len(near_two)),)),
                ],
            ),
            out_shape=[shape_of(rows, features), shape_of(rows, features)]
            + [shape_of(parts, 2, rows, width)]
            + [shape_of(parts, 2, count_rows, width, dtype=F32) for count_rows in (one, two)]
            + [shape_of(*far_back())]
            + [shape_of(2, two, width)] * len(near_two)
            + [shape_of(2, pack, width)] * 2,
            input_output_aliases={count + n: n for n in range(len(earlier))},
            compiler_params=params,
            cost_estimate=cost,
            name="attend",
        )(
            position,
            block_links.T,
            queries,
            out_grad,
            key_vecs,
            value_vecs,
            coarse_taps,
            one_in,
            two_in,
            *pair,
            *twos,
            far_in,
            *earlier,
        )

    def exchange_of(n):
        first, second, near = packs[3 * n : 3 * n + 3]
        return exchange([near] * len(near_two), first, second)

    twos, pair = exchange_of(0)
    if tm_count == 4:
        far_in = lax.ppermute(far, "tm", [(0, 3), (3, 0)])
    else:
        twos = twos[::-1]
        far_in = lax.all_gather(far, "tm")
    shared, returned = [], []
    for g in range(parts):
        if g + 1 < parts:
            pair, twos, far_in, later = lax.optimization_barrier(
                (pair, twos, far_in, tuple(packs[3 * g + 3 : 3 * g + 6]))
            )
            coming = exchange([later[2]] * len(near_two), later[0], later[1])
        pair = [pltpu.with_memory_space_constraint(x, pltpu.VMEM) for x in pair]
        outs = attend(g, level_one, packs[3 * g + 2], pair, twos, far_in, shared)
        shared = list(outs[:5])
        if g + 1 < parts:
            twos, pair = coming
        leaving = list(outs[5:])
        if g > 0:
            leaving, returned[-1] = lax.optimization_barrier((leaving, returned[-1]))
        near_in, pair_in = exchange(leaving[1:-2], leaving[-2], leaving[-1])
        if tm_count == 4:
            from_far = lax.ppermute(leaving[0], "tm", [(0, 3), (3, 0)])
        else:
            from_far = lax.psum_scatter(leaving[0], "tm", scatter_dimension=0)
        returned.append([*near_in, *pair_in, from_far])
    attended, grad_query, *owns = shared
    chunks = one // RIM

    def chunk_of(g, count):
        return pl.BlockSpec((None, 2, count // chunks, width), lambda c, *_: (g, 0, c, 0))

    def finish(g, earlier):
        count = 8 + len(near_two)
        return pl.pallas_call(
            lambda *refs: finish_kernel(len(near_two), *refs[:count], *refs[count + len(earlier) :]),
            grid_spec=pltpu.PrefetchScalarGridSpec(
                num_scalar_prefetch=1,
                grid=(chunks,),
                in_specs=[chunk_of(g, rows), chunk_of(g, one), chunk_of(g, two), lanes_of(g, 2, 4, 4)]
                + [whole(2, two, width)] * len(near_two)
                + [whole(2, pack, width)] * 2
                + [whole(2, three, width)]
                + [in_place] * len(earlier),
                out_specs=[pl.BlockSpec((rows // chunks, width), lambda c, *_: (c, g))] * 2,
                scratch_shapes=wide_scratch(rows // chunks, RIM, two)
                + [pltpu.VMEM((two, width), F32), pltpu.VMEM((2, 2 * RIM, width), BF16)],
            ),
            out_shape=[shape_of(rows, features)] * 2,
            input_output_aliases={count + n: n for n in range(len(earlier))},
            compiler_params=params,
            name="finish",
        )(position, *owns, coarse_taps, *returned[g], *earlier)

    grads = []
    for g in range(parts):
        grads = list(finish(g, grads))
    grad_key, grad_value = grads
    return tuple(x[None] for x in (attended, grad_query, grad_key, grad_value))


def solution(mesh):
    spec = P(("groups", "series"), "tm", "head")
    in_specs = (spec, spec, spec, spec, P("tm", None), P(None, None, None, "head"))
    return jax.shard_map(shards, mesh=mesh, in_specs=in_specs, out_specs=(spec,) * 4, check_vma=False)
```
